32 devices in a mesh: seq: 8 (over y, x, core), seg: 4 (over z).
Axes of the slice: x: 2, y: 2, z: 4, core: 2. Of those that a mesh axis runs over, the one named last changes fastest.
Arguments:
- query_rows: bfloat16 [4, 2048, 4, 128], P('seg', 'seq'), may hold values from -6 to 6
- key_rows: bfloat16 [4, 2048, 2, 4, 128], P('seg', 'seq'), may hold values from -6 to 6
- value_rows: bfloat16 [4, 2048, 2, 4, 128], P('seg', 'seq'), may hold values from -6 to 6
- out_gain: float32 [4, 128], replicated, may hold values from 0.5 to 1.5
- initial_state: float32 [4, 128, 128], replicated, may hold values from -24 to 24
Outputs:
- normed_out: bfloat16 [4, 2048, 4, 128], P('seg', 'seq')
The draws below stay inside these ranges and needn't reach their ends.
All inputs are finite; a program needn't handle non-finite values.
Results may differ from the reference program's by a relative error of at most 0.004.
Values sent between devices are 32-bit elements; how exact they have to be, the bound alone decides.
A program may use at most 128 MiB of HBM per device.

```python
import jax
import jax.numpy as jnp
from jax import lax

DK = 128
DV = 128
HEADS = 4
REFL = 2
GROUP = 128
SEGTOK = 2048
SEGS = 4


def steps_of(key, shape, pieces, low, top_value):
    loudness = 1.0
    for position, shards_of in pieces:
        heights = jax.random.uniform(jax.random.fold_in(jax.random.fold_in(key, 6), position), (shards_of,), jnp.float32, low / len(pieces), top_value / len(pieces))
        loudness = loudness * jnp.repeat(jnp.exp(heights), shape[position] // shards_of).reshape((-1,) + (1,) * (len(shape) - 1 - position))
    return loudness


def normal_values(rng, dims, spread, reach, split=(), kind=jnp.bfloat16):
    values = jax.random.normal(rng, dims, jnp.float32) * spread
    if len(split) > 0:
        values = steps_of(rng, dims, split, -0.22, 0.18) * values
    return jnp.clip(values, min=-reach, max=reach).astype(kind)


def setup_inputs(seed: int = 0) -> dict:
    key_list = jax.random.split(jax.random.key(seed), 6)
    return {
        "query_rows": normal_values(key_list[0], (SEGS, SEGTOK, HEADS, DK), 1.0, 6.0, ((0, 4), (1, 8))),
        "key_rows": normal_values(key_list[1], (SEGS, SEGTOK, REFL, HEADS, DK), 1.0, 6.0, ((0, 4), (1, 8))),
        "value_rows": normal_values(key_list[2], (SEGS, SEGTOK, REFL, HEADS, DV), 1.0, 6.0, ((0, 4), (1, 8))),
        "out_gain": jnp.clip(1.0 + 0.1 * jax.random.normal(key_list[3], (HEADS, DV), jnp.float32), 0.5, 1.5),
        "initial_state": normal_values(key_list[4], (HEADS, DK, DV), 4.0, 24.0, (), jnp.float32),
    }


highest = lax.Precision.HIGHEST

def unit_keys(raw):
    raw = raw.astype(jnp.float32)
    return raw * lax.rsqrt(lax.optimization_barrier(jnp.sum(raw * raw, axis=-1, keepdims=True)) + 1e-06)

def solve_single(matrix, target):
    return jax.scipy.linalg.solve_triangular(matrix, target, lower=True, unit_diagonal=True)

def block_factors(query, keyed, valued):
    steps = keyed.shape[-2]
    tokens = query.shape[-2]
    key_gram = jnp.einsum('...id,...jd->...ij', keyed, keyed, precision=highest)
    lower_unit = jnp.eye(steps, dtype=jnp.float32) + jnp.tril(2.0 * key_gram, -1)
    target = jnp.concatenate([2.0 * keyed, 2.0 * valued], axis=-1)
    flat_lower = lower_unit.reshape(-1, steps, steps)
    flat_target = target.reshape(-1, steps, target.shape[-1])
    solved = jax.vmap(solve_single)(flat_lower, flat_target).reshape(target.shape)
    weights = solved[..., :keyed.shape[-1]]
    updates = solved[..., keyed.shape[-1]:]
    visible = jnp.arange(steps)[None, :] <= REFL * jnp.arange(tokens)[:, None] + (REFL - 1)
    scores = jnp.where(visible, jnp.einsum('...td,...ld->...tl', query, keyed, precision=highest), 0.0)
    return (weights, updates, scores)

def reference(query_rows, key_rows, value_rows, out_gain, initial_state):
    total = query_rows.shape[0] * query_rows.shape[1]
    nblock = total // GROUP
    query = query_rows.astype(jnp.float32).reshape(nblock, GROUP, HEADS, DK).transpose(0, 2, 1, 3)
    keyed = unit_keys(key_rows).reshape(nblock, GROUP * REFL, HEADS, DK).transpose(0, 2, 1, 3)
    valued = value_rows.astype(jnp.float32).reshape(nblock, GROUP * REFL, HEADS, DV).transpose(0, 2, 1, 3)

    def advance(state, block):
        query_block, key_block, value_block = block
        weights, updates, scores = block_factors(query_block, key_block, value_block)
        residue = updates - jnp.einsum('hld,hde->hle', weights, state, precision=highest)
        read = jnp.einsum('htd,hde->hte', query_block, state, precision=highest)
        read = read + jnp.einsum('htl,hle->hte', scores, residue, precision=highest)
        state = state + jnp.einsum('hld,hle->hde', key_block, residue, precision=highest)
        return (state, read)
    final_state, reads = lax.scan(advance, initial_state.astype(jnp.float32), (query, keyed, valued))
    reads = reads.transpose(0, 2, 1, 3).reshape(query_rows.shape[0], query_rows.shape[1], HEADS, DV)
    scale = lax.rsqrt(lax.optimization_barrier(jnp.mean(reads * reads, axis=-1, keepdims=True)) + 1e-06)
    return (reads * scale * out_gain).astype(jnp.bfloat16)
```

```python
import functools

import jax
import jax.numpy as jnp
from jax import lax
from jax.experimental import pallas as pl
from jax.experimental.pallas import tpu as pltpu
from jax.sharding import PartitionSpec as P

F32 = jnp.float32
BF16 = jnp.bfloat16
REFL = 2
BLK = 128
SUB = 16
LANES = 128
MESH = pl.DeviceIdType.MESH


def dot(a, b):
    return lax.dot_general(a, b, (((1,), (0,)), ((), ())), preferred_element_type=F32)


def dot_bt(a, b):
    return lax.dot_general(a, b, (((1,), (1,)), ((), ())), preferred_element_type=F32)


def dot_at(a, b):
    return lax.dot_general(a, b, (((0,), (0,)), ((), ())), preferred_element_type=F32)


def split(x):
    high = x.astype(BF16)
    return high, (x - high.astype(F32)).astype(BF16)


def dot3(a, b):
    ah, al = a
    bh, bl = b
    rows, width = ah.shape[0], bh.shape[1]
    both = jnp.concatenate([ah, al], 0)
    if width <= LANES:
        full = dot(both, jnp.concatenate([bh, bl], 1))
        return full[:rows, :width] + (full[:rows, width:] + full[rows:, :width])
    full = dot(both, bh)
    return full[:rows] + (full[rows:] + dot(ah, bl))


def dot2(a, exact):
    rows = a[0].shape[0]
    full = dot(jnp.concatenate(a, 0), exact)
    return full[:rows] + full[rows:]


def iota(shape, axis):
    return lax.broadcasted_iota(jnp.int32, shape, axis)


def grouped(x, size, odd):
    return [x[g * size : (g + 1) * size] for g in range(odd, x.shape[0] // size, 2)]


def factors(first, per, heads, nblk, kf, vf, dsc, nsc, kb, scaled_hi, scaled_lo, before, pair):
    dk = kf.shape[1]
    row, col = iota((BLK, BLK), 0), iota((BLK, BLK), 1)
    eye = row == col
    lane = iota((SUB, BLK), 1)
    count = per * nblk

    keys, lowers, rcols, rrows = [], [], [], []
    for n in range(count):
        h, c = n // nblk, n % nblk
        key = kf[pl.ds(c * BLK * heads + first + h, BLK, stride=heads), :].astype(BF16)
        kb[first + h, c] = key
        gram = dot_bt(key, key)
        diag = jnp.where(eye, gram, 0.0)
        rcol = lax.rsqrt(jnp.sum(diag, axis=1, keepdims=True) + 1e-6)
        rrow = lax.rsqrt(jnp.sum(diag, axis=0, keepdims=True) + 1e-6)
        lower = jnp.where(row > col, gram * (2.0 * rcol) * rrow, 0.0)
        packed = lower[:SUB]
        for g in range(1, BLK // SUB):
            packed = jnp.where(lane // SUB == g, lower[g * SUB : (g + 1) * SUB], packed)
        dsc[n * SUB : (n + 1) * SUB, :] = packed
        keys.append(key)
        lowers.append(lower)
        rcols.append(rcol)
        rrows.append(rrow)

    lane_c = iota((count, BLK), 1)
    solved = []
    for i in range(SUB):
        line = dsc[pl.ds(i, count, stride=SUB), :]
        total = jnp.where(lane_c % SUB == i, 1.0, 0.0)
        for j in range(i):
            factor = jnp.take_along_axis(line, (lane_c // SUB) * SUB + j, axis=1)
            total = total - factor * solved[j]
        solved.append(total)
        nsc[pl.ds(i, count, stride=SUB), :] = total

    inverses = []
    for n in range(count):
        packed = nsc[n * SUB : (n + 1) * SUB, :]
        inverses.append(
            jnp.concatenate(
                [jnp.where(lane // SUB == g, packed, 0.0) for g in range(BLK // SUB)], axis=0
            )
        )
    half = BLK // 2
    size = SUB
    while size < BLK:
        paired = iota((half, BLK), 1) // size == 2 * (iota((half, BLK), 0) // size)
        for n in range(count):
            inv = split(inverses[n])
            odd = jnp.concatenate(grouped(lowers[n], size, 1), 0)
            part = dot3(split(jnp.where(paired, odd, 0.0)), inv)
            blank = jnp.zeros((size, BLK), F32)
            spread = []
            for g in range(half // size):
                spread += [blank, part[g * size : (g + 1) * size]]
            own = tuple(jnp.concatenate(grouped(x, size, 1), 0) for x in inv)
            fill = dot3(own, split(jnp.concatenate(spread, 0)))
            even, odd = grouped(inverses[n], size, 0), grouped(inverses[n], size, 1)
            rows = []
            for g in range(half // size):
                rows += [even[g], odd[g] - fill[g * size : (g + 1) * size]]
            inverses[n] = jnp.concatenate(rows, 0)
        size *= 2

    for h in range(per):
        trans = add = None
        for c in range(nblk):
            n = h * nblk + c
            key, rcol, rrow = keys[n], rcols[n], rrows[n]
            value = vf[pl.ds(c * BLK * heads + first + h, BLK, stride=heads), :].astype(BF16)
            weights = dot2(split(inverses[n] * (2.0 * rrow)), key)
            updates = dot2(split(inverses[n] * 2.0), value)
            scaled = split(jnp.concatenate([weights, updates], axis=1) * rcol)
            scaled_hi[first + h, c] = scaled[0]
            scaled_lo[first + h, c] = scaled[1]
            moved = dot_at(key, scaled[0]) + dot_at(key, scaled[1])
            step_trans = jnp.where(eye, 1.0, 0.0) - moved[:, :dk]
            step_add = moved[:, dk:]
            if c == 0:
                trans, add = step_trans, step_add
            else:
                so_far = jnp.concatenate([trans, add], axis=1)
                before[first + h, c] = so_far
                after = dot3(split(step_trans), split(so_far))
                trans, add = after[:, :dk], after[:, dk:] + step_add
        pair[first + h, :, :dk] = trans
        pair[first + h, :, dk:] = add


def readers(h, heads, nblk, qf, kb, scaled_hi, scaled_lo, before, reach, base):
    dk = qf.shape[1]
    tok = BLK // REFL
    visible = iota((tok, BLK), 1) <= REFL * iota((tok, BLK), 0) + (REFL - 1)
    for c in range(nblk):
        query = qf[pl.ds(c * tok * heads + h, tok, stride=heads), :]
        scores = jnp.where(visible, dot_bt(query.astype(BF16), kb[h, c]), 0.0)
        read = dot3(split(scores), (scaled_hi[h, c], scaled_lo[h, c]))
        project = query - read[:, :dk]
        local = read[:, dk:]
        rows = slice(c * tok, (c + 1) * tok)
        if c == 0:
            reach[h, rows, :] = project
            base[h, rows, :] = local
        else:
            gone = dot3(split(project), split(before[h, c]))
            reach[h, rows, :] = gone[:, :dk]
            base[h, rows, :] = gone[:, dk:] + local


def kernel(
    seqs, segs, heads, per,
    q_ref, k_ref, v_ref, gain_ref, init_ref, out_ref,
    qf, kf, vf, dsc, nsc, kb, scaled_hi, scaled_lo, before, pair, reach, base,
    rx, prefix, outgoing, total, tree, zx, first_state, zstate, own_state, state,
    put_sem, got_sem, zput_sem, zgot_sem, sput_sem, sgot_sem,
):
    dk = init_ref.shape[1]
    dv = init_ref.shape[2]
    nblk = k_ref.shape[0] // (heads * BLK)
    span = seqs // heads
    me = lax.axis_index("seq")
    seg = lax.axis_index("seg")
    owner = lax.rem(me, span) == 0
    mine = me // span

    barrier = pltpu.get_barrier_semaphore()
    for d in range(1, seqs):
        pl.semaphore_signal(
            barrier, inc=1,
            device_id={"seq": lax.rem(me + d, seqs), "seg": seg}, device_id_type=MESH,
        )
    for d in range(1, segs):
        pl.semaphore_signal(
            barrier, inc=1,
            device_id={"seq": me, "seg": lax.rem(seg + d, segs)}, device_id_type=MESH,
        )

    def copy(src, dst, put, got, to_seq, to_seg):
        return pltpu.make_async_remote_copy(
            src_ref=src, dst_ref=dst, send_sem=put, recv_sem=got,
            device_id={"seq": to_seq, "seg": to_seg}, device_id_type=MESH,
        )

    def put(h):
        return copy(pair.at[h], rx.at[me], put_sem.at[h], got_sem.at[me], h * span, seg)

    def got(s):
        return copy(rx.at[s], rx.at[s], put_sem.at[0], got_sem.at[s], s, seg)

    def sput(s):
        return copy(outgoing.at[s], own_state.at[mine], sput_sem.at[s], sgot_sem.at[mine], s, seg)

    def sgot(h):
        return copy(outgoing.at[0], own_state.at[h], sput_sem.at[0], sgot_sem.at[h], h * span, seg)

    def zput(g):
        return copy(tree.at[seqs - 2], zx.at[seg], zput_sem.at[g], zgot_sem.at[seg], me, g)

    def zgot(g):
        return copy(tree.at[seqs - 2], zx.at[g], zput_sem.at[g], zgot_sem.at[g], me, g)

    def fput(g):
        return copy(first_state, zstate, zput_sem.at[g], zgot_sem.at[0], me, g)

    kf[...] = k_ref[...].astype(F32)
    vf[...] = v_ref[...].astype(F32)
    qf[...] = q_ref[...].astype(F32)

    def local(i, _):
        turn = lax.rem(i + 1 + mine // per, heads // per)
        factors(turn * per, per, heads, nblk, kf, vf, dsc, nsc, kb, scaled_hi, scaled_lo, before, pair)

        @pl.when(i == 0)
        def _():
            pl.semaphore_wait(barrier, seqs + segs - 2)

        for d in range(per):
            h = turn * per + d

            @pl.when(me != h * span)
            def _():
                put(h).start()

        return 0

    lax.fori_loop(0, heads // per, local, 0)

    def reading(h, _):
        readers(h, heads, nblk, qf, kb, scaled_hi, scaled_lo, before, reach, base)
        return 0

    lax.fori_loop(0, heads, reading, 0)

    @pl.when(owner)
    def _():
        total[:, :dk] = jnp.where(iota((dk, dk), 0) == iota((dk, dk), 1), 1.0, 0.0).astype(F32)
        total[:, dk:] = jnp.zeros((dk, dv), F32)
        rx[me] = pair[mine]

        def arrived(s, _):
            @pl.when(s != me)
            def _():
                got(s).wait_recv()

            return 0

        lax.fori_loop(0, seqs, arrived, 0)
        parts = [rx.at[s] for s in range(seqs)]
        slot = 0
        while len(parts) > 1:
            joined = []
            for early, late in zip(parts[::2], parts[1::2]):
                after = dot3(split(late[:, :dk]), split(early[...]))
                tree[slot, :, :dk] = after[:, :dk]
                tree[slot, :, dk:] = after[:, dk:] + late[:, dk:]
                joined.append(tree.at[slot])
                slot += 1
            parts = joined + (parts[-1:] if len(parts) % 2 else [])

        @pl.when(seg == 0)
        def _():
            whole = tree[seqs - 2]
            first_state[...] = dot3(split(whole[:, :dk]), split(init_ref[mine])) + whole[:, dk:]
            for g in range(1, segs):
                fput(g).start()

        for g in range(2, segs):

            @pl.when((seg > 0) & (seg < g))
            def _():
                zput(g).start()

        def one(s, _):
            so_far = total[...]
            prefix[s] = so_far
            after = dot3(split(rx[s, :, :dk]), split(so_far))
            total[:, :dk] = after[:, :dk]
            total[:, dk:] = after[:, dk:] + rx[s, :, dk:]
            return 0

        lax.fori_loop(0, seqs, one, 0)

    @pl.when(owner)
    def _():
        @pl.when(seg == 0)
        def _():
            state[...] = init_ref[mine]

        @pl.when(seg > 0)
        def _():
            fput(0).wait_recv()
            state[...] = zstate[...]

        for g in range(1, segs - 1):

            @pl.when(g < seg)
            def _():
                zgot(g).wait_recv()
                state[...] = dot3(split(zx[g, :, :dk]), split(state[...])) + zx[g, :, dk:]

        def give(k, _):
            s = lax.rem(2 * seqs - 2 - me + k, seqs)
            ready = dot3(split(prefix[s, :, :dk]), split(state[...])) + prefix[s, :, dk:]

            @pl.when(s != me)
            def _():
                outgoing[s] = ready
                sput(s).start()

            @pl.when(s == me)
            def _():
                own_state[mine] = ready

            return 0

        lax.fori_loop(0, seqs, give, 0)

    for h in range(heads):

        @pl.when(me != h * span)
        def _():
            sgot(h).wait_recv()

        read = dot3(split(reach[h]), split(own_state[h])) + base[h]
        scale = lax.rsqrt(jnp.mean(read * read, axis=-1, keepdims=True) + 1e-6)
        normed = read * scale * gain_ref[h : h + 1, :]
        qf[pl.ds(h, read.shape[0], stride=heads), :] = normed
    out_ref[...] = qf[...].astype(BF16)

    for h in range(heads):

        @pl.when(me != h * span)
        def _():
            put(h).wait_send()

    @pl.when(owner)
    def _():
        @pl.when(seg == 0)
        def _():
            for g in range(1, segs):
                fput(g).wait_send()

        for g in range(2, segs):

            @pl.when((seg > 0) & (seg < g))
            def _():
                zput(g).wait_send()

        def done(s, _):
            @pl.when(s != me)
            def _():
                sput(s).wait_send()

            return 0

        lax.fori_loop(0, seqs, done, 0)


def per_device(seqs, segs, query_rows, key_rows, value_rows, out_gain, initial_state):
    _, tokens, heads, dk = query_rows.shape
    dv = value_rows.shape[-1]
    steps = tokens * REFL
    nblk = steps // BLK
    per = 2
    count = per * nblk
    wide = dk + dv
    vmem = pl.BlockSpec(memory_space=pltpu.VMEM)
    dma = pltpu.SemaphoreType.DMA
    out = pl.pallas_call(
        functools.partial(kernel, seqs, segs, heads, per),
        in_specs=[vmem] * 5,
        out_specs=vmem,
        out_shape=pltpu.VMEM((tokens * heads, dv), BF16),
        scratch_shapes=[
            pltpu.VMEM((tokens * heads, dk), F32),
            pltpu.VMEM((steps * heads, dk), F32),
            pltpu.VMEM((steps * heads, dv), F32),
            pltpu.VMEM((count * SUB, BLK), F32),
            pltpu.VMEM((count * SUB, BLK), F32),
            pltpu.VMEM((heads, nblk, BLK, dk), BF16),
            pltpu.VMEM((heads, nblk, BLK, wide), BF16),
            pltpu.VMEM((heads, nblk, BLK, wide), BF16),
            pltpu.VMEM((heads, nblk, dk, wide), F32),
            pltpu.VMEM((heads, dk, wide), F32),
            pltpu.VMEM((heads, tokens, dk), F32),
            pltpu.VMEM((heads, tokens, dv), F32),
            pltpu.VMEM((seqs, dk, wide), F32),
            pltpu.VMEM((seqs, dk, wide), F32),
            pltpu.VMEM((seqs, dk, dv), F32),
            pltpu.VMEM((dk, wide), F32),
            pltpu.VMEM((seqs - 1, dk, wide), F32),
            pltpu.VMEM((segs, dk, wide), F32),
            pltpu.VMEM((dk, dv), F32),
            pltpu.VMEM((dk, dv), F32),
            pltpu.VMEM((heads, dk, dv), F32),
            pltpu.VMEM((dk, dv), F32),
            dma((heads,)),
            dma((seqs,)),
            dma((segs,)),
            dma((segs,)),
            dma((seqs,)),
            dma((heads,)),
        ],
        compiler_params=pltpu.CompilerParams(collective_id=0, has_side_effects=True),
        name="delta_product",
    )(
        query_rows.reshape(tokens * heads, dk),
        key_rows.reshape(steps * heads, dk),
        value_rows.reshape(steps * heads, dv),
        out_gain,
        initial_state,
    )
    return out.reshape(1, tokens, heads, dv)


def solution(mesh):
    return jax.shard_map(
        functools.partial(per_device, mesh.shape["seq"], mesh.shape["seg"]),
        mesh=mesh,
        in_specs=(
            P("seg", "seq", None, None),
            P("seg", "seq", None, None, None),
            P("seg", "seq", None, None, None),
            P(),
            P(),
        ),
        out_specs=P("seg", "seq", None, None),
        check_vma=False,
    )
```

```python
import functools

import jax
import jax.numpy as jnp
from jax import lax
from jax.experimental import pallas as pl
from jax.experimental.pallas import tpu as pltpu
from jax.sharding import PartitionSpec as P

F32 = jnp.float32
BF16 = jnp.bfloat16
REFL = 2
BLK = 128
SUB = 16
LANES = 128
MESH = pl.DeviceIdType.MESH


def dot(a, b):
    return lax.dot_general(a, b, (((1,), (0,)), ((), ())), preferred_element_type=F32)


def dot_bt(a, b):
    return lax.dot_general(a, b, (((1,), (1,)), ((), ())), preferred_element_type=F32)


def dot_at(a, b):
    return lax.dot_general(a, b, (((0,), (0,)), ((), ())), preferred_element_type=F32)


def split(x):
    high = x.astype(BF16)
    return high, (x - high.astype(F32)).astype(BF16)


def dot3(a, b):
    ah, al = a
    bh, bl = b
    rows, width = ah.shape[0], bh.shape[1]
    both = jnp.concatenate([ah, al], 0)
    if width <= LANES:
        full = dot(both, jnp.concatenate([bh, bl], 1))
        return full[:rows, :width] + (full[:rows, width:] + full[rows:, :width])
    full = dot(both, bh)
    return full[:rows] + (full[rows:] + dot(ah, bl))


def dot2(a, exact):
    rows = a[0].shape[0]
    full = dot(jnp.concatenate(a, 0), exact)
    return full[:rows] + full[rows:]


def iota(shape, axis):
    return lax.broadcasted_iota(jnp.int32, shape, axis)


def grouped(x, size, odd):
    return [x[g * size : (g + 1) * size] for g in range(odd, x.shape[0] // size, 2)]


def invert_level(inv, low, size):
    half = BLK // 2
    paired = iota((half, BLK), 1) // size == 2 * (iota((half, BLK), 0) // size)
    high, rest = split(inv)
    under = jnp.where(paired, jnp.concatenate(grouped(low, size, 1), 0), 0.0)
    part = dot3(split(under), (high, rest))
    blank = jnp.zeros((size, BLK), F32)
    spread = []
    for g in range(half // size):
        spread += [blank, part[g * size : (g + 1) * size]]
    own = tuple(jnp.concatenate(grouped(x, size, 1), 0) for x in (high, rest))
    fill = dot3(own, split(jnp.concatenate(spread, 0)))
    even, odd = grouped(inv, size, 0), grouped(inv, size, 1)
    rows = []
    for g in range(half // size):
        rows += [even[g], odd[g] - fill[g * size : (g + 1) * size]]
    return jnp.concatenate(rows, 0)


def wide(x):
    return jnp.concatenate(split(x), 1)


def tall(x):
    return jnp.concatenate(split(x), 0)


def compose_split(left, right):
    lh, ll = left
    rh, rl = right
    return dot(jnp.concatenate([lh, ll], 1), jnp.concatenate([rh, rh], 0)) + dot(lh, rl)


def compose(left, right):
    return compose_split(split(left), split(right))


def grams(first, per, heads, nblk, kf, dsc, low, norm, kb):
    row, col = iota((BLK, BLK), 0), iota((BLK, BLK), 1)
    eye = row == col
    lane = iota((SUB, BLK), 1)
    count = per * nblk
    at = [(first + n // nblk, n % nblk) for n in range(count)]
    keys = [kf[pl.ds(c * BLK * heads + h, BLK, stride=heads), :].astype(BF16) for h, c in at]
    products = [dot_bt(key, key) for key in keys]
    diags = [jnp.where(eye, gram, 0.0) for gram in products]
    rcols = [lax.rsqrt(jnp.sum(diag, axis=1, keepdims=True) + 1e-6) for diag in diags]
    rrows = [lax.rsqrt(jnp.sum(diag, axis=0, keepdims=True) + 1e-6) for diag in diags]
    for n, (h, c) in enumerate(at):
        kb[h, c] = keys[n]
        norm[first * nblk + n] = rrows[n]
        lower = jnp.where(row > col, products[n] * (2.0 * rcols[n] * rcols[n]), 0.0)
        low[first * nblk + n] = lower
        packed = lower[:SUB]
        for g in range(1, BLK // SUB):
            packed = jnp.where(lane // SUB == g, lower[g * SUB : (g + 1) * SUB], packed)
        dsc[pl.ds(pl.multiple_of((first * nblk + n) * SUB, SUB), SUB), :] = packed


def substitute(count, dsc, nsc):
    lane = iota((count, BLK), 1)
    solved = []
    for i in range(SUB):
        line = dsc[pl.ds(i, count, stride=SUB), :]
        total = jnp.where(lane % SUB == i, 1.0, 0.0)
        for j in range(i):
            factor = jnp.take_along_axis(line, (lane // SUB) * SUB + j, axis=1)
            total = total - factor * solved[j]
        solved.append(total)
        nsc[pl.ds(i, count, stride=SUB), :] = total


def factors(first, per, heads, nblk, vf, nsc, low, norm, kb, scaled_hi, scaled_lo, before, pair):
    dk = kb.shape[-1]
    eye = iota((BLK, BLK), 0) == iota((BLK, BLK), 1)
    lane = iota((SUB, BLK), 1)
    inverses = []
    base = first * nblk
    for n in range(per * nblk):
        packed = nsc[pl.ds(pl.multiple_of((base + n) * SUB, SUB), SUB), :]
        inverses.append(
            jnp.concatenate(
                [jnp.where(lane // SUB == g, packed, 0.0) for g in range(BLK // SUB)], axis=0
            )
        )
    size = SUB
    while size < BLK:
        inverses = [invert_level(inv, low[base + n], size) for n, inv in enumerate(inverses)]
        size *= 2

    count = per * nblk
    at = [(first + n // nblk, n % nblk) for n in range(count)]
    keys = [kb[h, c] for h, c in at]
    keys = [jnp.concatenate([key, key], 0) for key in keys]
    values = [vf[pl.ds(c * BLK * heads + h, BLK, stride=heads), :].astype(BF16) for h, c in at]
    rrows = [norm[base + n] for n in range(count)]
    doubled = [inv * (2.0 * rrow) for inv, rrow in zip(inverses, rrows)]
    updates = [dot(wide(d), jnp.concatenate([v, v], 0)) for d, v in zip(doubled, values)]
    weights = [dot(wide(d * rrow), key) for d, rrow, key in zip(doubled, rrows, keys)]
    scaled = [split(jnp.concatenate([w, u], axis=1)) for w, u in zip(weights, updates)]
    moved = [dot_at(key, jnp.concatenate(s, 0)) for key, s in zip(keys, scaled)]
    for (h, c), s in zip(at, scaled):
        scaled_hi[h, c] = s[0]
        scaled_lo[h, c] = s[1]
    unit = jnp.where(eye, 1.0, 0.0)
    so_far = [
        jnp.concatenate([unit - moved[h * nblk][:, :dk], moved[h * nblk][:, dk:]], axis=1)
        for h in range(per)
    ]
    for c in range(1, nblk):
        for h in range(per):
            step = moved[h * nblk + c]
            before[first + h, c] = so_far[h]
            after = compose(unit - step[:, :dk], so_far[h])
            so_far[h] = jnp.concatenate([after[:, :dk], after[:, dk:] + step[:, dk:]], axis=1)
    for h in range(per):
        pair[first + h] = so_far[h]


def readers(h, heads, nblk, qf, kb, scaled_hi, scaled_lo, before, reach, base):
    dk = qf.shape[1]
    tok = BLK // REFL
    visible = iota((tok, BLK), 1) <= REFL * iota((tok, BLK), 0) + (REFL - 1)
    blocks = range(nblk)
    queries = [qf[pl.ds(c * tok * heads + h, tok, stride=heads), :] for c in blocks]
    scores = [dot_bt(queries[c].astype(BF16), kb[h, c]) for c in blocks]
    scores = [split(jnp.where(visible, score, 0.0)) for score in scores]
    reads = [compose_split(scores[c], (scaled_hi[h, c], scaled_lo[h, c])) for c in blocks]
    gone = [split(query - read[:, :dk]) for query, read in zip(queries, reads)]
    reach[h, :tok, :] = jnp.concatenate(gone[0], 1)
    base[h, :tok, :] = reads[0][:, dk:]
    for c in range(1, nblk):
        rows = slice(c * tok, (c + 1) * tok)
        moved = compose_split(gone[c], split(before[h, c]))
        reach[h, rows, :] = wide(moved[:, :dk])
        base[h, rows, :] = moved[:, dk:] + reads[c][:, dk:]


def kernel(
    seqs, segs, heads, per,
    q_any, k_any, v_any, gain_any, init_any, out_ref,
    q_ref, k_ref, v_ref, gain_ref, init_ref, in_sem,
    qf, kf, vf, dsc, nsc, low, norm, kb, scaled_hi, scaled_lo, before, pair, reach, base,
    rx, prefix, outgoing, total, tree, zx, first_state, zstate, own_state, state,
    put_sem, got_sem, zput_sem, zgot_sem, sput_sem, sgot_sem,
):
    dk = init_ref.shape[0]
    dv = init_ref.shape[1]
    nblk = k_ref.shape[0] // (heads * BLK)
    span = seqs // heads
    me = lax.axis_index("seq")
    seg = lax.axis_index("seg")
    owner = lax.rem(me, span) == 0
    mine = me // span

    loads = [
        pltpu.make_async_copy(src, dst, in_sem.at[i])
        for i, (src, dst) in enumerate(
            [
                (k_any, k_ref),
                (v_any, v_ref),
                (q_any, q_ref),
                (gain_any, gain_ref),
                (init_any.at[mine], init_ref),
            ]
        )
    ]
    for load in loads:
        load.start()
    barrier = pltpu.get_barrier_semaphore()
    for d in range(1, seqs):
        pl.semaphore_signal(
            barrier, inc=1,
            device_id={"seq": lax.rem(me + d, seqs), "seg": seg}, device_id_type=MESH,
        )
    for d in range(1, segs):
        pl.semaphore_signal(
            barrier, inc=1,
            device_id={"seq": me, "seg": lax.rem(seg + d, segs)}, device_id_type=MESH,
        )

    def copy(src, dst, put, got, to_seq, to_seg):
        return pltpu.make_async_remote_copy(
            src_ref=src, dst_ref=dst, send_sem=put, recv_sem=got,
            device_id={"seq": to_seq, "seg": to_seg}, device_id_type=MESH,
        )

    def put(h):
        return copy(pair.at[h], rx.at[me], put_sem.at[h], got_sem.at[me], h * span, seg)

    def got(s):
        return copy(rx.at[s], rx.at[s], put_sem.at[0], got_sem.at[s], s, seg)

    def sput(s):
        return copy(outgoing.at[s], own_state.at[mine], sput_sem.at[s], sgot_sem.at[mine], s, seg)

    def sgot(h):
        return copy(outgoing.at[0], own_state.at[h], sput_sem.at[0], sgot_sem.at[h], h * span, seg)

    def zput(g):
        return copy(tree.at[seqs - 2], zx.at[seg], zput_sem.at[g], zgot_sem.at[seg], me, g)

    def zgot(g):
        return copy(tree.at[seqs - 2], zx.at[g], zput_sem.at[g], zgot_sem.at[g], me, g)

    def fput(g):
        return copy(first_state, zstate, zput_sem.at[g], zgot_sem.at[0], me, g)

    loads[0].wait()
    kf[...] = k_ref[...].astype(F32)

    def gramming(i, _):
        grams(i * per, per, heads, nblk, kf, dsc, low, norm, kb)
        return 0

    lax.fori_loop(0, heads // per, gramming, 0)
    substitute(heads * nblk, dsc, nsc)
    for load in loads[1:]:
        load.wait()
    vf[...] = v_ref[...].astype(F32)
    qf[...] = q_ref[...].astype(F32)

    def local(i, _):
        turn = lax.rem(i + 1 + mine // per, heads // per)
        factors(turn * per, per, heads, nblk, vf, nsc, low, norm, kb, scaled_hi, scaled_lo, before, pair)

        @pl.when(i == 0)
        def _():
            pl.semaphore_wait(barrier, seqs + segs - 2)

        for d in range(per):
            h = turn * per + d

            @pl.when(me != h * span)
            def _():
                put(h).start()

        return 0

    lax.fori_loop(0, heads // per, local, 0)

    def reading(h, _):
        readers(h, heads, nblk, qf, kb, scaled_hi, scaled_lo, before, reach, base)
        return 0

    lax.fori_loop(0, heads, reading, 0)

    @pl.when(owner)
    def _():
        total[:, :dk] = jnp.where(iota((dk, dk), 0) == iota((dk, dk), 1), 1.0, 0.0).astype(F32)
        total[:, dk:] = jnp.zeros((dk, dv), F32)
        rx[me] = pair[mine]

        def arrived(s, _):
            @pl.when(s != me)
            def _():
                got(s).wait_recv()

            return 0

        lax.fori_loop(0, seqs, arrived, 0)
        parts = [rx.at[s] for s in range(seqs)]
        slot = 0
        while len(parts) > 1:
            joined = []
            for early, late in zip(parts[::2], parts[1::2]):
                after = dot3(split(late[:, :dk]), split(early[...]))
                tree[slot, :, :dk] = after[:, :dk]
                tree[slot, :, dk:] = after[:, dk:] + late[:, dk:]
                joined.append(tree.at[slot])
                slot += 1
            parts = joined + (parts[-1:] if len(parts) % 2 else [])

        @pl.when(seg == 0)
        def _():
            whole = tree[seqs - 2]
            first_state[...] = dot3(split(whole[:, :dk]), split(init_ref[...])) + whole[:, dk:]
            for g in range(segs - 1, 0, -1):
                fput(g).start()

        for g in range(segs - 1, 1, -1):

            @pl.when((seg > 0) & (seg < g))
            def _():
                zput(g).start()

        def one(s, _):
            so_far = total[...]
            prefix[s] = so_far
            after = dot3(split(rx[s, :, :dk]), split(so_far))
            total[:, :dk] = after[:, :dk]
            total[:, dk:] = after[:, dk:] + rx[s, :, dk:]
            return 0

        lax.fori_loop(0, seqs, one, 0)

    @pl.when(owner)
    def _():
        @pl.when(seg == 0)
        def _():
            state[...] = init_ref[...]

        @pl.when(seg > 0)
        def _():
            fput(0).wait_recv()
            state[...] = zstate[...]

        for g in range(1, segs - 1):

            @pl.when(g < seg)
            def _():
                zgot(g).wait_recv()
                state[...] = dot3(split(zx[g, :, :dk]), split(state[...])) + zx[g, :, dk:]

        def give(k, _):
            s = lax.rem(2 * seqs - 2 - me + k, seqs)
            ready = dot3(split(prefix[s, :, :dk]), split(state[...])) + prefix[s, :, dk:]

            @pl.when(s != me)
            def _():
                outgoing[s] = ready
                sput(s).start()

            @pl.when(s == me)
            def _():
                own_state[mine] = ready

            return 0

        lax.fori_loop(0, seqs, give, 0)

    for h in range(heads):

        @pl.when(me != h * span)
        def _():
            sgot(h).wait_recv()

    states = [split(own_state[h]) for h in range(heads)]
    reads = [
        dot(reach[h], jnp.concatenate([hi, hi], 0)) + dot(reach[h, :, :dk], lo) + base[h]
        for h, (hi, lo) in enumerate(states)
    ]
    squares = [jnp.mean(read * read, axis=-1, keepdims=True) for read in reads]
    for h, read in enumerate(reads):
        normed = read * lax.rsqrt(squares[h] + 1e-6) * gain_ref[h : h + 1, :]
        qf[pl.ds(h, read.shape[0], stride=heads), :] = normed
    out_ref[...] = qf[...].astype(BF16)

    for h in range(heads):

        @pl.when(me != h * span)
        def _():
            put(h).wait_send()

    @pl.when(owner)
    def _():
        @pl.when(seg == 0)
        def _():
            for g in range(1, segs):
                fput(g).wait_send()

        for g in range(2, segs):

            @pl.when((seg > 0) & (seg < g))
            def _():
                zput(g).wait_send()

        def done(s, _):
            @pl.when(s != me)
            def _():
                sput(s).wait_send()

            return 0

        lax.fori_loop(0, seqs, done, 0)


def per_device(seqs, segs, query_rows, key_rows, value_rows, out_gain, initial_state):
    _, tokens, heads, dk = query_rows.shape
    dv = value_rows.shape[-1]
    steps = tokens * REFL
    nblk = steps // BLK
    per = 2
    count = heads * nblk
    wide = dk + dv
    anywhere = pl.BlockSpec(memory_space=pl.ANY)
    vmem = pl.BlockSpec(memory_space=pltpu.VMEM)
    dma = pltpu.SemaphoreType.DMA
    out = pl.pallas_call(
        functools.partial(kernel, seqs, segs, heads, per),
        in_specs=[anywhere] * 5,
        out_specs=vmem,
        out_shape=pltpu.VMEM((tokens * heads, dv), BF16),
        scratch_shapes=[
            pltpu.VMEM((tokens * heads, dk), BF16),
            pltpu.VMEM((steps * heads, dk), BF16),
            pltpu.VMEM((steps * heads, dv), BF16),
            pltpu.VMEM((heads, dv), F32),
            pltpu.VMEM((dk, dv), F32),
            dma((5,)),
            pltpu.VMEM((tokens * heads, dk), F32),
            pltpu.VMEM((steps * heads, dk), F32),
            pltpu.VMEM((steps * heads, dv), F32),
            pltpu.VMEM((count * SUB, BLK), F32),
            pltpu.VMEM((count * SUB, BLK), F32),
            pltpu.VMEM((count, BLK, BLK), F32),
            pltpu.VMEM((count, 1, BLK), F32),
            pltpu.VMEM((heads, nblk, BLK, dk), BF16),
            pltpu.VMEM((heads, nblk, BLK, wide), BF16),
            pltpu.VMEM((heads, nblk, BLK, wide), BF16),
            pltpu.VMEM((heads, nblk, dk, wide), F32),
            pltpu.VMEM((heads, dk, wide), F32),
            pltpu.VMEM((heads, tokens, 2 * dk), BF16),
            pltpu.VMEM((heads, tokens, dv), F32),
            pltpu.VMEM((seqs, dk, wide), F32),
            pltpu.VMEM((seqs, dk, wide), F32),
            pltpu.VMEM((seqs, dk, dv), F32),
            pltpu.VMEM((dk, wide), F32),
            pltpu.VMEM((seqs - 1, dk, wide), F32),
            pltpu.VMEM((segs, dk, wide), F32),
            pltpu.VMEM((dk, dv), F32),
            pltpu.VMEM((dk, dv), F32),
            pltpu.VMEM((heads, dk, dv), F32),
            pltpu.VMEM((dk, dv), F32),
            dma((heads,)),
            dma((seqs,)),
            dma((segs,)),
            dma((segs,)),
            dma((seqs,)),
            dma((heads,)),
        ],
        compiler_params=pltpu.CompilerParams(collective_id=0, has_side_effects=True),
        name="delta_product",
    )(
        query_rows.reshape(tokens * heads, dk),
        key_rows.reshape(steps * heads, dk),
        value_rows.reshape(steps * heads, dv),
        out_gain,
        initial_state,
    )
    return out.reshape(1, tokens, heads, dv)


def solution(mesh):
    return jax.shard_map(
        functools.partial(per_device, mesh.shape["seq"], mesh.shape["seg"]),
        mesh=mesh,
        in_specs=(
            P("seg", "seq", None, None),
            P("seg", "seq", None, None, None),
            P("seg", "seq", None, None, None),
            P(),
            P(),
        ),
        out_specs=P("seg", "seq", None, None),
        check_vma=False,
    )
```

```python
import functools

import jax
import jax.numpy as jnp
from jax import lax
from jax.experimental import pallas as pl
from jax.experimental.pallas import tpu as pltpu
from jax.sharding import PartitionSpec as P

F32 = jnp.float32
BF16 = jnp.bfloat16
REFL = 2
CORES = 2
BLK = 128
SUB = 16
LANES = 128
MESH = pl.DeviceIdType.MESH


def dot(a, b):
    return lax.dot_general(a, b, (((1,), (0,)), ((), ())), preferred_element_type=F32)


def dot_bt(a, b):
    return lax.dot_general(a, b, (((1,), (1,)), ((), ())), preferred_element_type=F32)


def dot_at(a, b):
    return lax.dot_general(a, b, (((0,), (0,)), ((), ())), preferred_element_type=F32)


def split(x):
    high = x.astype(BF16)
    return high, (x - high.astype(F32)).astype(BF16)


def dot3(a, b):
    ah, al = a
    bh, bl = b
    rows, width = ah.shape[0], bh.shape[1]
    both = jnp.concatenate([ah, al], 0)
    if width <= LANES:
        full = dot(both, jnp.concatenate([bh, bl], 1))
        return full[:rows, :width] + (full[:rows, width:] + full[rows:, :width])
    full = dot(both, bh)
    return full[:rows] + (full[rows:] + dot(ah, bl))


def dot2(a, exact):
    rows = a[0].shape[0]
    full = dot(jnp.concatenate(a, 0), exact)
    return full[:rows] + full[rows:]


def iota(shape, axis):
    return lax.broadcasted_iota(jnp.int32, shape, axis)


def grouped(x, size, odd):
    return [x[g * size : (g + 1) * size] for g in range(odd, x.shape[0] // size, 2)]


def invert_level(inv, low, size):
    half = BLK // 2
    paired = iota((half, BLK), 1) // size == 2 * (iota((half, BLK), 0) // size)
    high, rest = split(inv)
    under = jnp.where(paired, jnp.concatenate(grouped(low, size, 1), 0), 0.0)
    part = dot3(split(under), (high, rest))
    blank = jnp.zeros((size, BLK), F32)
    spread = []
    for g in range(half // size):
        spread += [blank, part[g * size : (g + 1) * size]]
    own = tuple(jnp.concatenate(grouped(x, size, 1), 0) for x in (high, rest))
    fill = dot3(own, split(jnp.concatenate(spread, 0)))
    even, odd = grouped(inv, size, 0), grouped(inv, size, 1)
    rows = []
    for g in range(half // size):
        rows += [even[g], odd[g] - fill[g * size : (g + 1) * size]]
    return jnp.concatenate(rows, 0)


def wide(x):
    return jnp.concatenate(split(x), 1)


def tall(x):
    return jnp.concatenate(split(x), 0)


def compose_split(left, right):
    lh, ll = left
    rh, rl = right
    return dot(jnp.concatenate([lh, ll], 1), jnp.concatenate([rh, rh], 0)) + dot(lh, rl)


def compose(left, right):
    return compose_split(split(left), split(right))


def grams(first, per, heads, nblk, kf, dsc, low, norm, kb):
    row, col = iota((BLK, BLK), 0), iota((BLK, BLK), 1)
    eye = row == col
    lane = iota((SUB, BLK), 1)
    count = per * nblk
    at = [(first + n // nblk, n % nblk) for n in range(count)]
    keys = [kf[pl.ds(c * BLK * heads + h, BLK, stride=heads), :].astype(BF16) for h, c in at]
    products = [dot_bt(key, key) for key in keys]
    diags = [jnp.where(eye, gram, 0.0) for gram in products]
    rcols = [lax.rsqrt(jnp.sum(diag, axis=1, keepdims=True) + 1e-6) for diag in diags]
    rrows = [lax.rsqrt(jnp.sum(diag, axis=0, keepdims=True) + 1e-6) for diag in diags]
    for n, (h, c) in enumerate(at):
        kb[h, c] = keys[n]
        norm[first * nblk + n] = rrows[n]
        lower = jnp.where(row > col, products[n] * (2.0 * rcols[n] * rcols[n]), 0.0)
        low[first * nblk + n] = lower
        packed = lower[:SUB]
        for g in range(1, BLK // SUB):
            packed = jnp.where(lane // SUB == g, lower[g * SUB : (g + 1) * SUB], packed)
        dsc[pl.ds(pl.multiple_of((first * nblk + n) * SUB, SUB), SUB), :] = packed


def substitute(count, dsc, nsc):
    lane = iota((count, BLK), 1)
    solved = []
    for i in range(SUB):
        line = dsc[pl.ds(i, count, stride=SUB), :]
        total = jnp.where(lane % SUB == i, 1.0, 0.0)
        for j in range(i):
            factor = jnp.take_along_axis(line, (lane // SUB) * SUB + j, axis=1)
            total = total - factor * solved[j]
        solved.append(total)
        nsc[pl.ds(i, count, stride=SUB), :] = total


def factors(first, per, heads, nblk, vf, nsc, low, norm, kb, scaled_hi, scaled_lo, before, both, core):
    dk = kb.shape[-1]
    eye = iota((BLK, BLK), 0) == iota((BLK, BLK), 1)
    lane = iota((SUB, BLK), 1)
    inverses = []
    base = first * nblk
    for n in range(per * nblk):
        packed = nsc[pl.ds(pl.multiple_of((base + n) * SUB, SUB), SUB), :]
        inverses.append(
            jnp.concatenate(
                [jnp.where(lane // SUB == g, packed, 0.0) for g in range(BLK // SUB)], axis=0
            )
        )
    size = SUB
    while size < BLK:
        inverses = [invert_level(inv, low[base + n], size) for n, inv in enumerate(inverses)]
        size *= 2

    count = per * nblk
    at = [(first + n // nblk, n % nblk) for n in range(count)]
    keys = [kb[h, c] for h, c in at]
    keys = [jnp.concatenate([key, key], 0) for key in keys]
    values = [vf[pl.ds(c * BLK * heads + h, BLK, stride=heads), :].astype(BF16) for h, c in at]
    rrows = [norm[base + n] for n in range(count)]
    doubled = [inv * (2.0 * rrow) for inv, rrow in zip(inverses, rrows)]
    updates = [dot(wide(d), jnp.concatenate([v, v], 0)) for d, v in zip(doubled, values)]
    weights = [dot(wide(d * rrow), key) for d, rrow, key in zip(doubled, rrows, keys)]
    scaled = [split(jnp.concatenate([w, u], axis=1)) for w, u in zip(weights, updates)]
    moved = [dot_at(key, jnp.concatenate(s, 0)) for key, s in zip(keys, scaled)]
    for (h, c), s in zip(at, scaled):
        scaled_hi[h, c] = s[0]
        scaled_lo[h, c] = s[1]
    unit = jnp.where(eye, 1.0, 0.0)
    so_far = [
        jnp.concatenate([unit - moved[h * nblk][:, :dk], moved[h * nblk][:, dk:]], axis=1)
        for h in range(per)
    ]
    for c in range(1, nblk):
        for h in range(per):
            step = moved[h * nblk + c]
            before[first + h, c] = so_far[h]
            after = compose(unit - step[:, :dk], so_far[h])
            so_far[h] = jnp.concatenate([after[:, :dk], after[:, dk:] + step[:, dk:]], axis=1)
    for h in range(per):
        both[core, first + h] = so_far[h]


def readers(h, heads, nblk, qf, kb, scaled_hi, scaled_lo, before, reach, base):
    dk = qf.shape[1]
    tok = BLK // REFL
    visible = iota((tok, BLK), 1) <= REFL * iota((tok, BLK), 0) + (REFL - 1)
    blocks = range(nblk)
    queries = [qf[pl.ds(c * tok * heads + h, tok, stride=heads), :] for c in blocks]
    scores = [dot_bt(queries[c].astype(BF16), kb[h, c]) for c in blocks]
    scores = [split(jnp.where(visible, score, 0.0)) for score in scores]
    reads = [compose_split(scores[c], (scaled_hi[h, c], scaled_lo[h, c])) for c in blocks]
    gone = [split(query - read[:, :dk]) for query, read in zip(queries, reads)]
    reach[h, :tok, :] = jnp.concatenate(gone[0], 1)
    base[h, :tok, :] = reads[0][:, dk:]
    for c in range(1, nblk):
        rows = slice(c * tok, (c + 1) * tok)
        moved = compose_split(gone[c], split(before[h, c]))
        reach[h, rows, :] = wide(moved[:, :dk])
        base[h, rows, :] = moved[:, dk:] + reads[c][:, dk:]


def applied(step, state):
    dk = step.shape[0]
    return compose(step[:, :dk], state) + step[:, dk:]


def joined(late, early):
    dk = early.shape[0]
    after = compose(late[:, :dk], early)
    return jnp.concatenate([after[:, :dk], after[:, dk:] + late[:, dk:]], axis=1)


def folding(h, both, reach, base):
    dk = both.shape[2]
    moved = compose_split((reach[h, :, :dk], reach[h, :, dk:]), split(both[0, h]))
    reach[h] = wide(moved[:, :dk])
    base[h] = base[h] + moved[:, dk:]


def kernel(
    seqs, segs, heads, per,
    q_any, k_any, v_any, gain_any, init_any, out_ref,
    q_ref, k_ref, v_ref, gain_ref, init_ref, in_sem,
    qf, kf, vf, dsc, nsc, low, norm, kb, scaled_hi, scaled_lo, before, both, merged, reach, base,
    rx, prefix, outgoing, total, tree, zx, first_state, zstate, own_state, state,
    mput_sem, mgot_sem, put_sem, got_sem, zput_sem, zgot_sem, sput_sem, sgot_sem, rput_sem, rgot_sem,
):
    dk = init_ref.shape[0]
    dv = init_ref.shape[1]
    half = dk // CORES
    nblk = k_ref.shape[0] // (heads * BLK)
    span = seqs // heads
    chips = seqs // CORES
    me = lax.axis_index("seq")
    seg = lax.axis_index("seg")
    core = lax.rem(me, CORES)
    chip = me // CORES
    mate = me + 1 - 2 * core
    owner = lax.rem(me, span) == 0
    mine = me // span
    mine_rows = pl.ds(pl.multiple_of(core * half, half), half)

    loads = [
        pltpu.make_async_copy(src, dst, in_sem.at[i])
        for i, (src, dst) in enumerate(
            [
                (k_any, k_ref),
                (v_any, v_ref),
                (q_any, q_ref),
                (gain_any, gain_ref),
                (init_any.at[mine], init_ref),
            ]
        )
    ]
    for load in loads:
        load.start()
    barrier = pltpu.get_barrier_semaphore()
    for d in range(1, seqs):
        pl.semaphore_signal(
            barrier, inc=1,
            device_id={"seq": lax.rem(me + d, seqs), "seg": seg}, device_id_type=MESH,
        )
    for d in range(1, segs):
        pl.semaphore_signal(
            barrier, inc=1,
            device_id={"seq": me, "seg": lax.rem(seg + d, segs)}, device_id_type=MESH,
        )

    def copy(src, dst, put, got, to_seq, to_seg):
        return pltpu.make_async_remote_copy(
            src_ref=src, dst_ref=dst, send_sem=put, recv_sem=got,
            device_id={"seq": to_seq, "seg": to_seg}, device_id_type=MESH,
        )

    def mput(h, c):
        ref = both.at[c, h] if c == 0 else both.at[c, h, :half]
        return copy(ref, ref, mput_sem.at[h], mgot_sem.at[h], mate, seg)

    def for_core(action):
        for c in range(CORES):

            @pl.when(core == c)
            def _():
                action(c)

    def put(h):
        return copy(
            merged.at[h], rx.at[chip, mine_rows], put_sem.at[h], got_sem.at[chip, core], h * span, seg
        )

    def got(s, c):
        ref = rx.at[s, pl.ds(c * half, half)]
        return copy(ref, ref, put_sem.at[0], got_sem.at[s, c], s * CORES, seg)

    def sput(s):
        return copy(
            outgoing.at[s], own_state.at[mine], sput_sem.at[s], sgot_sem.at[mine], s * CORES, seg
        )

    def sgot(h):
        return copy(own_state.at[h], own_state.at[h], sput_sem.at[0], sgot_sem.at[h], h * span, seg)

    def rput(h):
        return copy(own_state.at[h], own_state.at[h], rput_sem.at[h], rgot_sem.at[h], mate, seg)

    def zput(g):
        return copy(tree.at[chips - 2], zx.at[seg], zput_sem.at[g], zgot_sem.at[seg], me, g)

    def zgot(g):
        return copy(tree.at[chips - 2], zx.at[g], zput_sem.at[g], zgot_sem.at[g], me, g)

    def fput(g):
        return copy(first_state, zstate, zput_sem.at[g], zgot_sem.at[0], me, g)

    loads[0].wait()
    kf[...] = k_ref[...].astype(F32)

    def gramming(i, _):
        grams(i * per, per, heads, nblk, kf, dsc, low, norm, kb)
        return 0

    lax.fori_loop(0, heads // per, gramming, 0)
    substitute(heads * nblk, dsc, nsc)
    for load in loads[1:]:
        load.wait()
    vf[...] = v_ref[...].astype(F32)
    qf[...] = q_ref[...].astype(F32)

    def group_of(i):
        turn = lax.rem(i + 1 + mine // per, heads // per)
        return turn, [turn * per + lax.rem(mine + 1 + d, per) for d in range(per)]

    def local(i, _):
        turn, group = group_of(i)
        factors(turn * per, per, heads, nblk, vf, nsc, low, norm, kb, scaled_hi, scaled_lo, before, both, core)

        @pl.when(i == 0)
        def _():
            pl.semaphore_wait(barrier, seqs + segs - 2)

        def exchange(c):
            for h in group:
                mput(h, c).start()

        for_core(exchange)
        return 0

    lax.fori_loop(0, heads // per, local, 0)

    def merging(i, _):
        _, group = group_of(i)

        def arrived(c):
            for h in group:
                mput(h, 1 - c).wait_recv()

        for_core(arrived)
        results = [joined(both[1, h, mine_rows], both[0, h]) for h in group]
        for h, result in zip(group, results):
            merged[h] = result

            @pl.when(me != h * span)
            def _():
                put(h).start()

            @pl.when(me == h * span)
            def _():
                rx[chip, mine_rows] = merged[h]

        return 0

    lax.fori_loop(0, heads // per, merging, 0)

    def reading(h, _):
        readers(h, heads, nblk, qf, kb, scaled_hi, scaled_lo, before, reach, base)
        return 0

    lax.fori_loop(0, heads, reading, 0)

    @pl.when(core > 0)
    def _():
        def fold(h, _):
            folding(h, both, reach, base)
            return 0

        lax.fori_loop(0, heads, fold, 0)

    @pl.when(owner)
    def _():
        def arrived(s, _):
            for c in range(CORES):

                @pl.when(s * CORES + c != me)
                def _():
                    got(s, c).wait_recv()

            return 0

        lax.fori_loop(0, chips, arrived, 0)
        parts = [rx.at[s] for s in range(chips)]
        slot = 0
        while len(parts) > 1:
            pairs = list(zip(parts[::2], parts[1::2]))
            results = [joined(late[...], early[...]) for early, late in pairs]
            fresh = []
            for result in results:
                tree[slot] = result
                fresh.append(tree.at[slot])
                slot += 1
            parts = fresh + (parts[-1:] if len(parts) % 2 else [])

        @pl.when(seg == 0)
        def _():
            first_state[...] = applied(tree[chips - 2], init_ref[...])
            for g in range(segs - 1, 0, -1):
                fput(g).start()

        for g in range(segs - 1, 1, -1):

            @pl.when((seg > 0) & (seg < g))
            def _():
                zput(g).start()

        total[:, :dk] = jnp.where(iota((dk, dk), 0) == iota((dk, dk), 1), 1.0, 0.0).astype(F32)
        total[:, dk:] = jnp.zeros((dk, dv), F32)

        def one(s, _):
            so_far = total[...]
            prefix[s] = so_far
            total[...] = joined(rx[s], so_far)
            return 0

        lax.fori_loop(0, chips, one, 0)

        @pl.when(seg == 0)
        def _():
            state[...] = init_ref[...]

        @pl.when(seg > 0)
        def _():
            fput(0).wait_recv()
            state[...] = zstate[...]

        for g in range(1, segs - 1):

            @pl.when(g < seg)
            def _():
                zgot(g).wait_recv()
                state[...] = applied(zx[g], state[...])

        def give(k, _):
            s = lax.rem(2 * chips - 1 - chip + k, chips)
            ready = applied(prefix[s], state[...])

            @pl.when(s != chip)
            def _():
                outgoing[s] = ready
                sput(s).start()

            @pl.when(s == chip)
            def _():
                own_state[mine] = ready

            return 0

        lax.fori_loop(0, chips, give, 0)

    @pl.when(core == 0)
    def _():
        def relay(k, _):
            h = lax.rem(mine + (k // per) + (k % per) * (heads // per), heads)

            @pl.when(me != h * span)
            def _():
                sgot(h).wait_recv()

            rput(h).start()
            return 0

        lax.fori_loop(0, heads, relay, 0)

    @pl.when(core > 0)
    def _():
        for h in range(heads):
            rput(h).wait_recv()

    states = [split(own_state[h]) for h in range(heads)]
    reads = [
        dot(reach[h], jnp.concatenate([hi, hi], 0)) + dot(reach[h, :, :dk], lo) + base[h]
        for h, (hi, lo) in enumerate(states)
    ]
    squares = [jnp.mean(read * read, axis=-1, keepdims=True) for read in reads]
    for h, read in enumerate(reads):
        normed = read * lax.rsqrt(squares[h] + 1e-6) * gain_ref[h : h + 1, :]
        qf[pl.ds(h, read.shape[0], stride=heads), :] = normed
    out_ref[...] = qf[...].astype(BF16)

    def sent(c):
        for h in range(heads):
            mput(h, c).wait_send()

    for_core(sent)

    for h in range(heads):

        @pl.when(me != h * span)
        def _():
            put(h).wait_send()

        @pl.when(core == 0)
        def _():
            rput(h).wait_send()

    @pl.when(owner)
    def _():
        @pl.when(seg == 0)
        def _():
            for g in range(1, segs):
                fput(g).wait_send()

        for g in range(2, segs):

            @pl.when((seg > 0) & (seg < g))
            def _():
                zput(g).wait_send()

        def done(s, _):
            @pl.when(s != chip)
            def _():
                sput(s).wait_send()

            return 0

        lax.fori_loop(0, chips, done, 0)


def per_device(seqs, segs, query_rows, key_rows, value_rows, out_gain, initial_state):
    _, tokens, heads, dk = query_rows.shape
    dv = value_rows.shape[-1]
    steps = tokens * REFL
    nblk = steps // BLK
    per = 2
    count = heads * nblk
    wide = dk + dv
    chips = seqs // CORES
    anywhere = pl.BlockSpec(memory_space=pl.ANY)
    vmem = pl.BlockSpec(memory_space=pltpu.VMEM)
    dma = pltpu.SemaphoreType.DMA
    out = pl.pallas_call(
        functools.partial(kernel, seqs, segs, heads, per),
        in_specs=[anywhere] * 5,
        out_specs=vmem,
        out_shape=pltpu.VMEM((tokens * heads, dv), BF16),
        scratch_shapes=[
            pltpu.VMEM((tokens * heads, dk), BF16),
            pltpu.VMEM((steps * heads, dk), BF16),
            pltpu.VMEM((steps * heads, dv), BF16),
            pltpu.VMEM((heads, dv), F32),
            pltpu.VMEM((dk, dv), F32),
            dma((5,)),
            pltpu.VMEM((tokens * heads, dk), F32),
            pltpu.VMEM((steps * heads, dk), F32),
            pltpu.VMEM((steps * heads, dv), F32),
            pltpu.VMEM((count * SUB, BLK), F32),
            pltpu.VMEM((count * SUB, BLK), F32),
            pltpu.VMEM((count, BLK, BLK), F32),
            pltpu.VMEM((count, 1, BLK), F32),
            pltpu.VMEM((heads, nblk, BLK, dk), BF16),
            pltpu.VMEM((heads, nblk, BLK, wide), BF16),
            pltpu.VMEM((heads, nblk, BLK, wide), BF16),
            pltpu.VMEM((heads, nblk, dk, wide), F32),
            pltpu.VMEM((CORES, heads, dk, wide), F32),
            pltpu.VMEM((heads, dk // CORES, wide), F32),
            pltpu.VMEM((heads, tokens, 2 * dk), BF16),
            pltpu.VMEM((heads, tokens, dv), F32),
            pltpu.VMEM((chips, dk, wide), F32),
            pltpu.VMEM((chips, dk, wide), F32),
            pltpu.VMEM((chips, dk, dv), F32),
            pltpu.VMEM((dk, wide), F32),
            pltpu.VMEM((chips - 1, dk, wide), F32),
            pltpu.VMEM((segs, dk, wide), F32),
            pltpu.VMEM((dk, dv), F32),
            pltpu.VMEM((dk, dv), F32),
            pltpu.VMEM((heads, dk, dv), F32),
            pltpu.VMEM((dk, dv), F32),
            dma((heads,)),
            dma((heads,)),
            dma((heads,)),
            dma((chips, CORES)),
            dma((segs,)),
            dma((segs,)),
            dma((chips,)),
            dma((heads,)),
            dma((heads,)),
            dma((heads,)),
        ],
        compiler_params=pltpu.CompilerParams(collective_id=0, has_side_effects=True),
        name="delta_product",
    )(
        query_rows.reshape(tokens * heads, dk),
        key_rows.reshape(steps * heads, dk),
        value_rows.reshape(steps * heads, dv),
        out_gain,
        initial_state,
    )
    return out.reshape(1, tokens, heads, dv)


def solution(mesh):
    return jax.shard_map(
        functools.partial(per_device, mesh.shape["seq"], mesh.shape["seg"]),
        mesh=mesh,
        in_specs=(
            P("seg", "seq", None, None),
            P("seg", "seq", None, None, None),
            P("seg", "seq", None, None, None),
            P(),
            P(),
        ),
        out_specs=P("seg", "seq", None, None),
        check_vma=False,
    )
```

```python
import functools

import jax
import jax.numpy as jnp
from jax import lax
from jax.experimental import pallas as pl
from jax.experimental.pallas import tpu as pltpu
from jax.sharding import PartitionSpec as P

F32 = jnp.float32
BF16 = jnp.bfloat16
REFL = 2
CORES = 2
BLK = 128
SUB = 16
LANES = 128
MESH = pl.DeviceIdType.MESH


def dot(a, b):
    return lax.dot_general(a, b, (((1,), (0,)), ((), ())), preferred_element_type=F32)


def dot_bt(a, b):
    return lax.dot_general(a, b, (((1,), (1,)), ((), ())), preferred_element_type=F32)


def dot_at(a, b):
    return lax.dot_general(a, b, (((0,), (0,)), ((), ())), preferred_element_type=F32)


def split(x):
    high = x.astype(BF16)
    return high, (x - high.astype(F32)).astype(BF16)


def dot3(a, b):
    ah, al = a
    bh, bl = b
    rows, width = ah.shape[0], bh.shape[1]
    both = jnp.concatenate([ah, al], 0)
    if width <= LANES:
        full = dot(both, jnp.concatenate([bh, bl], 1))
        return full[:rows, :width] + (full[:rows, width:] + full[rows:, :width])
    full = dot(both, bh)
    return full[:rows] + (full[rows:] + dot(ah, bl))


def dot2(a, exact):
    rows = a[0].shape[0]
    full = dot(jnp.concatenate(a, 0), exact)
    return full[:rows] + full[rows:]


def iota(shape, axis):
    return lax.broadcasted_iota(jnp.int32, shape, axis)


def grouped(x, size, odd):
    return [x[g * size : (g + 1) * size] for g in range(odd, x.shape[0] // size, 2)]


def joined(late, early):
    dk = early.shape[0]
    after = compose(late[:, :dk], early)
    return jnp.concatenate([after[:, :dk], after[:, dk:] + late[:, dk:]], axis=1)


def invert_level(inv, low, size):
    half = BLK // 2
    paired = iota((half, BLK), 1) // size == 2 * (iota((half, BLK), 0) // size)
    high, rest = split(inv)
    under = jnp.where(paired, jnp.concatenate(grouped(low, size, 1), 0), 0.0)
    if 2 * size == BLK:
        part = dot3(split(under[:, :size]), (high[:size], rest[:size]))
    else:
        part = dot3(split(under), (high, rest))
    blank = jnp.zeros((size, BLK), F32)
    spread = []
    for g in range(half // size):
        spread += [blank, part[g * size : (g + 1) * size]]
    own = tuple(jnp.concatenate(grouped(x, size, 1), 0) for x in (high, rest))
    fill = dot3(own, split(jnp.concatenate(spread, 0)))
    even, odd = grouped(inv, size, 0), grouped(inv, size, 1)
    rows = []
    for g in range(half // size):
        rows += [even[g], odd[g] - fill[g * size : (g + 1) * size]]
    return jnp.concatenate(rows, 0)


def wide(x):
    return jnp.concatenate(split(x), 1)


def tall(x):
    return jnp.concatenate(split(x), 0)


def compose_split(left, right):
    lh, ll = left
    rh, rl = right
    return dot(jnp.concatenate([lh, ll], 1), jnp.concatenate([rh, rh], 0)) + dot(lh, rl)


def compose(left, right):
    return compose_split(split(left), split(right))


def grams(first, per, heads, nblk, kf, dsc, low, norm, kb):
    row, col = iota((BLK, BLK), 0), iota((BLK, BLK), 1)
    eye = row == col
    lane = iota((SUB, BLK), 1)
    count = per * nblk
    at = [(first + n // nblk, n % nblk) for n in range(count)]
    keys = [kf[pl.ds(c * BLK * heads + h, BLK, stride=heads), :].astype(BF16) for h, c in at]
    products = [dot_bt(key, key) for key in keys]
    diags = [jnp.where(eye, gram, 0.0) for gram in products]
    rcols = [lax.rsqrt(jnp.sum(diag, axis=1, keepdims=True) + 1e-6) for diag in diags]
    rrows = [lax.rsqrt(jnp.sum(diag, axis=0, keepdims=True) + 1e-6) for diag in diags]
    for n, (h, c) in enumerate(at):
        kb[h, c] = keys[n]
        norm[first * nblk + n] = rrows[n]
        lower = jnp.where(row > col, products[n] * (2.0 * rcols[n] * rcols[n]), 0.0)
        low[first * nblk + n] = lower
        packed = lower[:SUB]
        for g in range(1, BLK // SUB):
            packed = jnp.where(lane // SUB == g, lower[g * SUB : (g + 1) * SUB], packed)
        dsc[pl.ds(pl.multiple_of((first * nblk + n) * SUB, SUB), SUB), :] = packed


def substitute(count, dsc, nsc):
    lane = iota((count, BLK), 1)
    solved = []
    for i in range(SUB):
        line = dsc[pl.ds(i, count, stride=SUB), :]
        total = jnp.where(lane % SUB == i, 1.0, 0.0)
        for j in range(i):
            factor = jnp.take_along_axis(line, (lane // SUB) * SUB + j, axis=1)
            total = total - factor * solved[j]
        solved.append(total)
        nsc[pl.ds(i, count, stride=SUB), :] = total


def factors(first, per, heads, nblk, vf, nsc, low, norm, kb, steps, scaled_hi, scaled_lo, before, both, core):
    dk = kb.shape[-1]
    eye = iota((BLK, BLK), 0) == iota((BLK, BLK), 1)
    lane = iota((SUB, BLK), 1)
    inverses = []
    base = first * nblk
    for n in range(per * nblk):
        packed = nsc[pl.ds(pl.multiple_of((base + n) * SUB, SUB), SUB), :]
        inverses.append(
            jnp.concatenate(
                [jnp.where(lane // SUB == g, packed, 0.0) for g in range(BLK // SUB)], axis=0
            )
        )
    size = SUB
    while size < BLK:
        inverses = [invert_level(inv, low[base + n], size) for n, inv in enumerate(inverses)]
        size *= 2

    count = per * nblk
    at = [(first + n // nblk, n % nblk) for n in range(count)]
    keys = [kb[h, c] for h, c in at]
    keys = [jnp.concatenate([key, key], 0) for key in keys]
    values = [vf[pl.ds(c * BLK * heads + h, BLK, stride=heads), :].astype(BF16) for h, c in at]
    rrows = [norm[base + n] for n in range(count)]
    doubled = [inv * (2.0 * rrow) for inv, rrow in zip(inverses, rrows)]
    updates = [dot(wide(d), jnp.concatenate([v, v], 0)) for d, v in zip(doubled, values)]
    weights = [dot(wide(d * rrow), key) for d, rrow, key in zip(doubled, rrows, keys)]
    scaled = [split(jnp.concatenate([w, u], axis=1)) for w, u in zip(weights, updates)]
    moved = [dot_at(key, jnp.concatenate(s, 0)) for key, s in zip(keys, scaled)]
    for (h, c), s in zip(at, scaled):
        scaled_hi[h, c] = s[0]
        scaled_lo[h, c] = s[1]
    unit = jnp.where(eye, 1.0, 0.0)
    nodes = [jnp.concatenate([unit - m[:, :dk], m[:, dk:]], axis=1) for m in moved]
    for n, (h, c) in enumerate(at):
        if c & (c + 1):
            steps[h, c] = nodes[n]
    nodes = [nodes[h * nblk : (h + 1) * nblk] for h in range(per)]
    reached = 1
    while len(nodes[0]) > 1:
        for h in range(per):
            before[first + h, reached] = nodes[h][0]
        nodes = [[joined(late, early) for early, late in zip(x[::2], x[1::2])] for x in nodes]
        reached *= 2
    for h in range(per):
        both[core, first + h] = nodes[h][0]


def readers(h, heads, nblk, qf, kb, steps, scaled_hi, scaled_lo, before, reach, base):
    dk = qf.shape[1]
    tok = BLK // REFL
    visible = iota((tok, BLK), 1) <= REFL * iota((tok, BLK), 0) + (REFL - 1)
    blocks = range(nblk)
    queries = [qf[pl.ds(c * tok * heads + h, tok, stride=heads), :] for c in blocks]
    scores = [dot_bt(queries[c].astype(BF16), kb[h, c]) for c in blocks]
    scores = [split(jnp.where(visible, score, 0.0)) for score in scores]
    reads = [compose_split(scores[c], (scaled_hi[h, c], scaled_lo[h, c])) for c in blocks]
    gone = [split(query - read[:, :dk]) for query, read in zip(queries, reads)]
    reach[h, :tok, :] = jnp.concatenate(gone[0], 1)
    base[h, :tok, :] = reads[0][:, dk:]
    so_far = None
    for c in range(1, nblk):
        rows = slice(c * tok, (c + 1) * tok)
        so_far = joined(steps[h, c - 1], so_far) if c & (c - 1) else before[h, c]
        moved = compose_split(gone[c], split(so_far))
        reach[h, rows, :] = wide(moved[:, :dk])
        base[h, rows, :] = moved[:, dk:] + reads[c][:, dk:]


def applied(step, state):
    dk = step.shape[0]
    return compose(step[:, :dk], state) + step[:, dk:]


def folding(h, both, reach, base):
    dk = both.shape[2]
    moved = compose_split((reach[h, :, :dk], reach[h, :, dk:]), split(both[0, h]))
    reach[h] = wide(moved[:, :dk])
    base[h] = base[h] + moved[:, dk:]


def kernel(
    seqs, segs, heads, per,
    q_any, k_any, v_any, gain_any, init_any, out_ref,
    q_ref, k_ref, v_ref, gain_ref, init_ref, in_sem,
    qf, kf, vf, dsc, nsc, low, norm, kb, steps, scaled_hi, scaled_lo, before, both, merged, reach, base,
    rx, prefix, outgoing, total, tree, zx, first_state, zstate, own_state, state,
    mput_sem, mgot_sem, put_sem, got_sem, zput_sem, zgot_sem, sput_sem, sgot_sem, rput_sem, rgot_sem,
):
    dk = init_ref.shape[0]
    dv = init_ref.shape[1]
    half = dk // CORES
    nblk = k_ref.shape[0] // (heads * BLK)
    span = seqs // heads
    chips = seqs // CORES
    me = lax.axis_index("seq")
    seg = lax.axis_index("seg")
    core = lax.rem(me, CORES)
    chip = me // CORES
    mate = me + 1 - 2 * core
    owner = lax.rem(me, span) == 0
    mine = me // span
    mine_rows = pl.ds(pl.multiple_of(core * half, half), half)

    def near(first, second):
        return (first != second) & ((first // 2 == second // 2) | (first % 2 == second % 2))

    def relayed(h):
        return jnp.logical_not(near(h * span // CORES, chip))

    loads = [
        pltpu.make_async_copy(src, dst, in_sem.at[i])
        for i, (src, dst) in enumerate(
            [
                (k_any, k_ref),
                (v_any, v_ref),
                (q_any, q_ref),
                (gain_any, gain_ref),
                (init_any.at[mine], init_ref),
            ]
        )
    ]
    for load in loads:
        load.start()
    barrier = pltpu.get_barrier_semaphore()
    for d in range(1, seqs):
        pl.semaphore_signal(
            barrier, inc=1,
            device_id={"seq": lax.rem(me + d, seqs), "seg": seg}, device_id_type=MESH,
        )
    for d in range(1, segs):
        pl.semaphore_signal(
            barrier, inc=1,
            device_id={"seq": me, "seg": lax.rem(seg + d, segs)}, device_id_type=MESH,
        )

    def copy(src, dst, put, got, to_seq, to_seg):
        return pltpu.make_async_remote_copy(
            src_ref=src, dst_ref=dst, send_sem=put, recv_sem=got,
            device_id={"seq": to_seq, "seg": to_seg}, device_id_type=MESH,
        )

    def mput(h, c):
        ref = both.at[c, h] if c == 0 else both.at[c, h, :half]
        return copy(ref, ref, mput_sem.at[h], mgot_sem.at[h], mate, seg)

    def for_core(action):
        for c in range(CORES):

            @pl.when(core == c)
            def _():
                action(c)

    def put(h):
        return copy(
            merged.at[h], rx.at[chip, mine_rows], put_sem.at[h], got_sem.at[chip, core], h * span, seg
        )

    def got(s, c):
        ref = rx.at[s, pl.ds(c * half, half)]
        return copy(ref, ref, put_sem.at[0], got_sem.at[s, c], s * CORES, seg)

    def sput(s, c):
        return copy(
            outgoing.at[s], own_state.at[mine], sput_sem.at[s, c], sgot_sem.at[mine], s * CORES + c, seg
        )

    def sgot(h):
        return copy(own_state.at[h], own_state.at[h], sput_sem.at[0, 0], sgot_sem.at[h], h * span, seg)

    def rput(h):
        return copy(own_state.at[h], own_state.at[h], rput_sem.at[h], rgot_sem.at[h], mate, seg)

    def zput(g):
        return copy(tree.at[chips - 2], zx.at[seg], zput_sem.at[g], zgot_sem.at[seg], me, g)

    def zgot(g):
        return copy(tree.at[chips - 2], zx.at[g], zput_sem.at[g], zgot_sem.at[g], me, g)

    def fput(g):
        return copy(first_state, zstate, zput_sem.at[g], zgot_sem.at[0], me, g)

    loads[0].wait()
    kf[...] = k_ref[...].astype(F32)

    def gramming(i, _):
        grams(i * per, per, heads, nblk, kf, dsc, low, norm, kb)
        return 0

    lax.fori_loop(0, heads // per, gramming, 0)
    substitute(heads * nblk, dsc, nsc)
    for load in loads[1:]:
        load.wait()
    vf[...] = v_ref[...].astype(F32)
    qf[...] = q_ref[...].astype(F32)

    def group_of(i):
        turn = lax.rem(i + 1 + mine // per, heads // per)
        return turn, [turn * per + lax.rem(mine + 1 + d, per) for d in range(per)]

    def local(i, _):
        turn, group = group_of(i)
        factors(turn * per, per, heads, nblk, vf, nsc, low, norm, kb, steps, scaled_hi, scaled_lo, before, both, core)

        @pl.when(i == 0)
        def _():
            pl.semaphore_wait(barrier, seqs + segs - 2)

        def exchange(c):
            for h in group:
                mput(h, c).start()

        for_core(exchange)
        return 0

    lax.fori_loop(0, heads // per, local, 0)

    def merging(i, _):
        _, group = group_of(i)

        def arrived(c):
            for h in group:
                mput(h, 1 - c).wait_recv()

        for_core(arrived)
        results = [joined(both[1, h, mine_rows], both[0, h]) for h in group]
        for h, result in zip(group, results):
            merged[h] = result

            @pl.when(me != h * span)
            def _():
                put(h).start()

            @pl.when(me == h * span)
            def _():
                rx[chip, mine_rows] = merged[h]

        return 0

    lax.fori_loop(0, heads // per, merging, 0)

    def reading(h, _):
        readers(h, heads, nblk, qf, kb, steps, scaled_hi, scaled_lo, before, reach, base)
        return 0

    lax.fori_loop(0, heads, reading, 0)

    @pl.when(core > 0)
    def _():
        def fold(h, _):
            folding(h, both, reach, base)
            return 0

        lax.fori_loop(0, heads, fold, 0)

    @pl.when(owner)
    def _():
        def arrived(s, _):
            for c in range(CORES):

                @pl.when(s * CORES + c != me)
                def _():
                    got(s, c).wait_recv()

            return 0

        lax.fori_loop(0, chips, arrived, 0)
        parts = [rx.at[s] for s in range(chips)]
        slot = 0
        while len(parts) > 1:
            pairs = list(zip(parts[::2], parts[1::2]))
            results = [joined(late[...], early[...]) for early, late in pairs]
            fresh = []
            for result in results:
                tree[slot] = result
                fresh.append(tree.at[slot])
                slot += 1
            parts = fresh + (parts[-1:] if len(parts) % 2 else [])

        @pl.when(seg == 0)
        def _():
            first_state[...] = applied(tree[chips - 2], init_ref[...])
            for g in range(segs - 1, 0, -1):
                fput(g).start()

        for g in range(segs - 1, 1, -1):

            @pl.when((seg > 0) & (seg < g))
            def _():
                zput(g).start()

        total[:, :dk] = jnp.where(iota((dk, dk), 0) == iota((dk, dk), 1), 1.0, 0.0).astype(F32)
        total[:, dk:] = jnp.zeros((dk, dv), F32)

        def one(s, _):
            so_far = total[...]
            prefix[s] = so_far
            total[...] = joined(rx[s], so_far)
            return 0

        lax.fori_loop(0, chips, one, 0)

        @pl.when(seg == 0)
        def _():
            state[...] = init_ref[...]

        @pl.when(seg > 0)
        def _():
            fput(0).wait_recv()
            state[...] = zstate[...]

        for g in range(1, segs - 1):

            @pl.when(g < seg)
            def _():
                zgot(g).wait_recv()
                state[...] = applied(zx[g], state[...])

        def give(k, _):
            s = lax.rem(2 * chips - 1 - chip + k, chips)
            ready = applied(prefix[s], state[...])

            @pl.when(s != chip)
            def _():
                outgoing[s] = ready
                sput(s, 0).start()

            @pl.when(near(s, chip))
            def _():
                sput(s, 1).start()

            @pl.when(s == chip)
            def _():
                own_state[mine] = ready

            return 0

        lax.fori_loop(0, chips, give, 0)

    def ordered(k):
        return lax.rem(mine + (k // per) + (k % per) * (heads // per), heads)

    @pl.when(core == 0)
    def _():
        for k in range(heads):
            h = ordered(k)

            @pl.when(me != h * span)
            def _():
                sgot(h).wait_recv()

            @pl.when(relayed(h))
            def _():
                rput(h).start()

    def closing(i, _):
        group = [ordered(i * 2 + d) for d in range(2)]

        @pl.when(core > 0)
        def _():
            for h in group:

                @pl.when(relayed(h))
                def _():
                    rput(h).wait_recv()

                @pl.when(jnp.logical_not(relayed(h)))
                def _():
                    sgot(h).wait_recv()

        states = [split(own_state[h]) for h in group]
        reads = [
            dot(reach[h], jnp.concatenate([hi, hi], 0)) + dot(reach[h, :, :dk], lo) + base[h]
            for h, (hi, lo) in zip(group, states)
        ]
        squares = [jnp.mean(read * read, axis=-1, keepdims=True) for read in reads]
        for h, read, square in zip(group, reads, squares):
            normed = read * lax.rsqrt(square + 1e-6) * gain_ref[pl.ds(h, 1), :]
            qf[pl.ds(h, read.shape[0], stride=heads), :] = normed
        return 0

    lax.fori_loop(0, heads // 2, closing, 0)
    out_ref[...] = qf[...].astype(BF16)

    def sent(c):
        for h in range(heads):
            mput(h, c).wait_send()

    for_core(sent)

    for h in range(heads):

        @pl.when(me != h * span)
        def _():
            put(h).wait_send()

        @pl.when((core == 0) & relayed(h))
        def _():
            rput(h).wait_send()

    @pl.when(owner)
    def _():
        @pl.when(seg == 0)
        def _():
            for g in range(1, segs):
                fput(g).wait_send()

        for g in range(2, segs):

            @pl.when((seg > 0) & (seg < g))
            def _():
                zput(g).wait_send()

        def done(s, _):
            @pl.when(s != chip)
            def _():
                sput(s, 0).wait_send()

            @pl.when(near(s, chip))
            def _():
                sput(s, 1).wait_send()

            return 0

        lax.fori_loop(0, chips, done, 0)


def per_device(seqs, segs, query_rows, key_rows, value_rows, out_gain, initial_state):
    _, tokens, heads, dk = query_rows.shape
    dv = value_rows.shape[-1]
    steps = tokens * REFL
    nblk = steps // BLK
    per = 2
    count = heads * nblk
    wide = dk + dv
    chips = seqs // CORES
    anywhere = pl.BlockSpec(memory_space=pl.ANY)
    vmem = pl.BlockSpec(memory_space=pltpu.VMEM)
    dma = pltpu.SemaphoreType.DMA
    out = pl.pallas_call(
        functools.partial(kernel, seqs, segs, heads, per),
        in_specs=[anywhere] * 5,
        out_specs=vmem,
        out_shape=pltpu.VMEM((tokens * heads, dv), BF16),
        scratch_shapes=[
            pltpu.VMEM((tokens * heads, dk), BF16),
            pltpu.VMEM((steps * heads, dk), BF16),
            pltpu.VMEM((steps * heads, dv), BF16),
            pltpu.VMEM((heads, dv), F32),
            pltpu.VMEM((dk, dv), F32),
            dma((5,)),
            pltpu.VMEM((tokens * heads, dk), F32),
            pltpu.VMEM((steps * heads, dk), F32),
            pltpu.VMEM((steps * heads, dv), F32),
            pltpu.VMEM((count * SUB, BLK), F32),
            pltpu.VMEM((count * SUB, BLK), F32),
            pltpu.VMEM((count, BLK, BLK), F32),
            pltpu.VMEM((count, 1, BLK), F32),
            pltpu.VMEM((heads, nblk, BLK, dk), BF16),
            pltpu.VMEM((heads, nblk, dk, wide), F32),
            pltpu.VMEM((heads, nblk, BLK, wide), BF16),
            pltpu.VMEM((heads, nblk, BLK, wide), BF16),
            pltpu.VMEM((heads, nblk, dk, wide), F32),
            pltpu.VMEM((CORES, heads, dk, wide), F32),
            pltpu.VMEM((heads, dk // CORES, wide), F32),
            pltpu.VMEM((heads, tokens, 2 * dk), BF16),
            pltpu.VMEM((heads, tokens, dv), F32),
            pltpu.VMEM((chips, dk, wide), F32),
            pltpu.VMEM((chips, dk, wide), F32),
            pltpu.VMEM((chips, dk, dv), F32),
            pltpu.VMEM((dk, wide), F32),
            pltpu.VMEM((chips - 1, dk, wide), F32),
            pltpu.VMEM((segs, dk, wide), F32),
            pltpu.VMEM((dk, dv), F32),
            pltpu.VMEM((dk, dv), F32),
            pltpu.VMEM((heads, dk, dv), F32),
            pltpu.VMEM((dk, dv), F32),
            dma((heads,)),
            dma((heads,)),
            dma((heads,)),
            dma((chips, CORES)),
            dma((segs,)),
            dma((segs,)),
            dma((chips, CORES)),
            dma((heads,)),
            dma((heads,)),
            dma((heads,)),
        ],
        compiler_params=pltpu.CompilerParams(collective_id=0, has_side_effects=True),
        name="delta_product",
    )(
        query_rows.reshape(tokens * heads, dk),
        key_rows.reshape(steps * heads, dk),
        value_rows.reshape(steps * heads, dv),
        out_gain,
        initial_state,
    )
    return out.reshape(1, tokens, heads, dv)


def solution(mesh):
    return jax.shard_map(
        functools.partial(per_device, mesh.shape["seq"], mesh.shape["seg"]),
        mesh=mesh,
        in_specs=(
            P("seg", "seq", None, None),
            P("seg", "seq", None, None, None),
            P("seg", "seq", None, None, None),
            P(),
            P(),
        ),
        out_specs=P("seg", "seq", None, None),
        check_vma=False,
    )
```

```python
import functools

import jax
import jax.numpy as jnp
from jax import lax
from jax.experimental import pallas as pl
from jax.experimental.pallas import tpu as pltpu
from jax.sharding import PartitionSpec as P

F32 = jnp.float32
BF16 = jnp.bfloat16
REFL = 2
CORES = 2
BLK = 128
SUB = 16
LANES = 128
MESH = pl.DeviceIdType.MESH


def dot(a, b):
    return lax.dot_general(a, b, (((1,), (0,)), ((), ())), preferred_element_type=F32)


def dot_bt(a, b):
    return lax.dot_general(a, b, (((1,), (1,)), ((), ())), preferred_element_type=F32)


def dot_at(a, b):
    return lax.dot_general(a, b, (((0,), (0,)), ((), ())), preferred_element_type=F32)


def split(x):
    high = x.astype(BF16)
    return high, (x - high.astype(F32)).astype(BF16)


def dot3(a, b):
    ah, al = a
    bh, bl = b
    rows, width = ah.shape[0], bh.shape[1]
    both = jnp.concatenate([ah, al], 0)
    if width <= LANES:
        full = dot(both, jnp.concatenate([bh, bl], 1))
        return full[:rows, :width] + (full[:rows, width:] + full[rows:, :width])
    full = dot(both, bh)
    return full[:rows] + (full[rows:] + dot(ah, bl))


def dot2(a, exact):
    rows = a[0].shape[0]
    full = dot(jnp.concatenate(a, 0), exact)
    return full[:rows] + full[rows:]


def iota(shape, axis):
    return lax.broadcasted_iota(jnp.int32, shape, axis)


def grouped(x, size, odd):
    return [x[g * size : (g + 1) * size] for g in range(odd, x.shape[0] // size, 2)]


def joined(late, early):
    dk = early.shape[0]
    after = compose(late[:, :dk], early)
    return jnp.concatenate([after[:, :dk], after[:, dk:] + late[:, dk:]], axis=1)


def invert_level(inv, low, size):
    half = BLK // 2
    paired = iota((half, BLK), 1) // size == 2 * (iota((half, BLK), 0) // size)
    high, rest = split(inv)
    under = jnp.where(paired, jnp.concatenate(grouped(low, size, 1), 0), 0.0)
    if 2 * size == BLK:
        part = dot3(split(under[:, :size]), (high[:size], rest[:size]))
    else:
        part = dot3(split(under), (high, rest))
    blank = jnp.zeros((size, BLK), F32)
    spread = []
    for g in range(half // size):
        spread += [blank, part[g * size : (g + 1) * size]]
    own = tuple(jnp.concatenate(grouped(x, size, 1), 0) for x in (high, rest))
    fill = dot3(own, split(jnp.concatenate(spread, 0)))
    even, odd = grouped(inv, size, 0), grouped(inv, size, 1)
    rows = []
    for g in range(half // size):
        rows += [even[g], odd[g] - fill[g * size : (g + 1) * size]]
    return jnp.concatenate(rows, 0)


def wide(x):
    return jnp.concatenate(split(x), 1)


def tall(x):
    return jnp.concatenate(split(x), 0)


def compose_split(left, right):
    lh, ll = left
    rh, rl = right
    return dot(jnp.concatenate([lh, ll], 1), jnp.concatenate([rh, rh], 0)) + dot(lh, rl)


def compose(left, right):
    return compose_split(split(left), split(right))


def grams(first, per, heads, nblk, kf, dsc, low, norm, kb):
    row, col = iota((BLK, BLK), 0), iota((BLK, BLK), 1)
    eye = row == col
    lane = iota((SUB, BLK), 1)
    at = [(first + n // nblk, n % nblk) for n in range(per * nblk)]
    products, squares = [], []
    for n, (h, c) in enumerate(at):
        key = kf[pl.ds(c * BLK * heads + h, BLK, stride=heads), :].astype(BF16)
        kb[h, c] = key
        products.append(dot_bt(key, key))
        yield
    for n, gram in enumerate(products):
        diag = jnp.where(eye, gram, 0.0)
        squares.append(jnp.sum(diag, axis=1, keepdims=True))
        norm[first * nblk + n] = lax.rsqrt(jnp.sum(diag, axis=0, keepdims=True) + 1e-6)
        yield
    for n, gram in enumerate(products):
        rcol = lax.rsqrt(squares[n] + 1e-6)
        lower = jnp.where(row > col, gram * (2.0 * rcol * rcol), 0.0)
        low[first * nblk + n] = lower
        packed = lower[:SUB]
        for g in range(1, BLK // SUB):
            packed = jnp.where(lane // SUB == g, lower[g * SUB : (g + 1) * SUB], packed)
        dsc[pl.ds(pl.multiple_of((first * nblk + n) * SUB, SUB), SUB), :] = packed
        yield


def substitute(first, count, dsc, nsc):
    lane = iota((count, BLK), 1)
    solved = []
    for i in range(SUB):
        line = dsc[pl.ds(first * SUB + i, count, stride=SUB), :]
        total = jnp.where(lane % SUB == i, 1.0, 0.0)
        for j in range(i):
            factor = jnp.take_along_axis(line, (lane // SUB) * SUB + j, axis=1)
            total = total - factor * solved[j]
        solved.append(total)
        nsc[pl.ds(first * SUB + i, count, stride=SUB), :] = total
        yield


def factors(beside, first, per, heads, nblk, vf, nsc, low, norm, kb, steps, scaled_hi, scaled_lo, before, both, core):
    dk = kb.shape[-1]
    eye = iota((BLK, BLK), 0) == iota((BLK, BLK), 1)
    lane = iota((SUB, BLK), 1)
    inverses = []
    base = first * nblk
    for n in range(per * nblk):
        packed = nsc[pl.ds(pl.multiple_of((base + n) * SUB, SUB), SUB), :]
        inverses.append(
            jnp.concatenate(
                [jnp.where(lane // SUB == g, packed, 0.0) for g in range(BLK // SUB)], axis=0
            )
        )
    size = SUB
    while size < BLK:
        for n in range(per * nblk):
            inverses[n] = invert_level(inverses[n], low[base + n], size)
            for _ in range(2):
                next(beside, None)
        size *= 2
    for _ in beside:
        pass

    count = per * nblk
    at = [(first + n // nblk, n % nblk) for n in range(count)]
    keys = [kb[h, c] for h, c in at]
    keys = [jnp.concatenate([key, key], 0) for key in keys]
    values = [vf[pl.ds(c * BLK * heads + h, BLK, stride=heads), :].astype(BF16) for h, c in at]
    rrows = [norm[base + n] for n in range(count)]
    doubled = [inv * (2.0 * rrow) for inv, rrow in zip(inverses, rrows)]
    updates = [dot(wide(d), jnp.concatenate([v, v], 0)) for d, v in zip(doubled, values)]
    weights = [dot(wide(d * rrow), key) for d, rrow, key in zip(doubled, rrows, keys)]
    scaled = [split(jnp.concatenate([w, u], axis=1)) for w, u in zip(weights, updates)]
    moved = [dot_at(key, jnp.concatenate(s, 0)) for key, s in zip(keys, scaled)]
    for (h, c), s in zip(at, scaled):
        scaled_hi[h, c] = s[0]
        scaled_lo[h, c] = s[1]
    unit = jnp.where(eye, 1.0, 0.0)
    nodes = [jnp.concatenate([unit - m[:, :dk], m[:, dk:]], axis=1) for m in moved]
    for n, (h, c) in enumerate(at):
        if c & (c + 1):
            steps[h, c] = nodes[n]
    nodes = [nodes[h * nblk : (h + 1) * nblk] for h in range(per)]
    reached = 1
    while len(nodes[0]) > 1:
        for h in range(per):
            before[first + h, reached] = nodes[h][0]
        nodes = [[joined(late, early) for early, late in zip(x[::2], x[1::2])] for x in nodes]
        reached *= 2
    for h in range(per):
        both[core, first + h] = nodes[h][0]


def readers(h, heads, nblk, qf, kb, steps, scaled_hi, scaled_lo, before, reach, base):
    dk = qf.shape[1]
    tok = BLK // REFL
    visible = iota((tok, BLK), 1) <= REFL * iota((tok, BLK), 0) + (REFL - 1)
    blocks = range(nblk)
    queries = [qf[pl.ds(c * tok * heads + h, tok, stride=heads), :] for c in blocks]
    scores = [dot_bt(queries[c].astype(BF16), kb[h, c]) for c in blocks]
    scores = [split(jnp.where(visible, score, 0.0)) for score in scores]
    reads = [compose_split(scores[c], (scaled_hi[h, c], scaled_lo[h, c])) for c in blocks]
    gone = [split(query - read[:, :dk]) for query, read in zip(queries, reads)]
    reach[h, :tok, :] = jnp.concatenate(gone[0], 1)
    base[h, :tok, :] = reads[0][:, dk:]
    so_far = None
    for c in range(1, nblk):
        rows = slice(c * tok, (c + 1) * tok)
        so_far = joined(steps[h, c - 1], so_far) if c & (c - 1) else before[h, c]
        moved = compose_split(gone[c], split(so_far))
        reach[h, rows, :] = wide(moved[:, :dk])
        base[h, rows, :] = moved[:, dk:] + reads[c][:, dk:]


def applied(step, state):
    dk = step.shape[0]
    return compose(step[:, :dk], state) + step[:, dk:]


def folding(h, both, reach, base):
    dk = both.shape[2]
    moved = compose_split((reach[h, :, :dk], reach[h, :, dk:]), split(both[0, h]))
    reach[h] = wide(moved[:, :dk])
    base[h] = base[h] + moved[:, dk:]


def kernel(
    seqs, segs, heads, per,
    q_any, k_any, v_any, gain_any, init_any, out_ref,
    q_ref, k_ref, v_ref, gain_ref, init_ref, in_sem,
    qf, kf, vf, dsc, nsc, low, norm, kb, steps, scaled_hi, scaled_lo, before, both, merged, reach, base,
    rx, prefix, outgoing, total, tree, zx, first_state, zstate, own_state, state,
    mput_sem, mgot_sem, put_sem, got_sem, zput_sem, zgot_sem, sput_sem, sgot_sem, rput_sem, rgot_sem,
):
    dk = init_ref.shape[0]
    dv = init_ref.shape[1]
    half = dk // CORES
    nblk = k_ref.shape[0] // (heads * BLK)
    span = seqs // heads
    chips = seqs // CORES
    me = lax.axis_index("seq")
    seg = lax.axis_index("seg")
    core = lax.rem(me, CORES)
    chip = me // CORES
    mate = me + 1 - 2 * core
    owner = lax.rem(me, span) == 0
    mine = me // span
    mine_rows = pl.ds(pl.multiple_of(core * half, half), half)

    def near(first, second):
        return (first != second) & ((first // 2 == second // 2) | (first % 2 == second % 2))

    def relayed(h):
        return jnp.logical_not(near(h * span // CORES, chip))

    loads = [
        pltpu.make_async_copy(src, dst, in_sem.at[i])
        for i, (src, dst) in enumerate(
            [
                (k_any, k_ref),
                (v_any, v_ref),
                (q_any, q_ref),
                (gain_any, gain_ref),
                (init_any.at[mine], init_ref),
            ]
        )
    ]
    for load in loads:
        load.start()
    barrier = pltpu.get_barrier_semaphore()
    for d in range(1, seqs):
        pl.semaphore_signal(
            barrier, inc=1,
            device_id={"seq": lax.rem(me + d, seqs), "seg": seg}, device_id_type=MESH,
        )
    for d in range(1, segs):
        pl.semaphore_signal(
            barrier, inc=1,
            device_id={"seq": me, "seg": lax.rem(seg + d, segs)}, device_id_type=MESH,
        )

    def copy(src, dst, put, got, to_seq, to_seg):
        return pltpu.make_async_remote_copy(
            src_ref=src, dst_ref=dst, send_sem=put, recv_sem=got,
            device_id={"seq": to_seq, "seg": to_seg}, device_id_type=MESH,
        )

    def mput(h, c):
        ref = both.at[c, h] if c == 0 else both.at[c, h, :half]
        return copy(ref, ref, mput_sem.at[h], mgot_sem.at[h], mate, seg)

    def for_core(action):
        for c in range(CORES):

            @pl.when(core == c)
            def _():
                action(c)

    def put(h):
        return copy(
            merged.at[h], rx.at[chip, mine_rows], put_sem.at[h], got_sem.at[chip, core], h * span, seg
        )

    def got(s, c):
        ref = rx.at[s, pl.ds(c * half, half)]
        return copy(ref, ref, put_sem.at[0], got_sem.at[s, c], s * CORES, seg)

    def sput(s, c):
        return copy(
            outgoing.at[s], own_state.at[mine], sput_sem.at[s, c], sgot_sem.at[mine], s * CORES + c, seg
        )

    def sgot(h):
        return copy(own_state.at[h], own_state.at[h], sput_sem.at[0, 0], sgot_sem.at[h], h * span, seg)

    def rput(h):
        return copy(own_state.at[h], own_state.at[h], rput_sem.at[h], rgot_sem.at[h], mate, seg)

    def zput(g):
        return copy(tree.at[chips - 2], zx.at[seg], zput_sem.at[g], zgot_sem.at[seg], me, g)

    def zgot(g):
        return copy(tree.at[chips - 2], zx.at[g], zput_sem.at[g], zgot_sem.at[g], me, g)

    def fput(g):
        return copy(first_state, zstate, zput_sem.at[g], zgot_sem.at[0], me, g)

    loads[0].wait()
    kf[...] = k_ref[...].astype(F32)

    def group_of(i):
        turn = lax.rem(i + 1 + mine // per, heads // per)
        return turn, [turn * per + lax.rem(mine + 1 + d, per) for d in range(per)]

    def prepared(first):
        yield from grams(first, per, heads, nblk, kf, dsc, low, norm, kb)
        yield from substitute(first * nblk, per * nblk, dsc, nsc)

    for _ in prepared(group_of(0)[0] * per):
        pass

    for load in loads[1:]:
        load.wait()
    vf[...] = v_ref[...].astype(F32)

    def local(i, _):
        turn, group = group_of(i)
        beside = prepared(group_of(i + 1)[0] * per)
        factors(beside, turn * per, per, heads, nblk, vf, nsc, low, norm, kb, steps, scaled_hi, scaled_lo, before, both, core)

        @pl.when(i == 0)
        def _():
            pl.semaphore_wait(barrier, seqs + segs - 2)

        def exchange(c):
            for h in group:
                mput(h, c).start()

        for_core(exchange)
        return 0

    lax.fori_loop(0, heads // per, local, 0)

    def merging(group):
        def arrived(c):
            for h in group:
                mput(h, 1 - c).wait_recv()

        for_core(arrived)
        results = [joined(both[1, h, mine_rows], both[0, h]) for h in group]
        for h, result in zip(group, results):
            merged[h] = result

            @pl.when(me != h * span)
            def _():
                put(h).start()

            @pl.when(me == h * span)
            def _():
                rx[chip, mine_rows] = merged[h]

    def merging_all(i, _):
        merging(group_of(i)[1])
        return 0

    lax.fori_loop(0, heads // per - 1, merging_all, 0)

    def merging_one(d, _):
        merging([group_of(heads // per - 1)[0] * per + lax.rem(mine + 1 + d, per)])
        return 0

    lax.fori_loop(0, per, merging_one, 0)

    qf[...] = q_ref[...].astype(F32)

    def reading(h, _):
        readers(h, heads, nblk, qf, kb, steps, scaled_hi, scaled_lo, before, reach, base)
        return 0

    lax.fori_loop(0, heads, reading, 0)

    @pl.when(core > 0)
    def _():
        def fold(h, _):
            folding(h, both, reach, base)
            return 0

        lax.fori_loop(0, heads, fold, 0)

    @pl.when(owner)
    def _():
        def arrived(s, _):
            for c in range(CORES):

                @pl.when(s * CORES + c != me)
                def _():
                    got(s, c).wait_recv()

            return 0

        lax.fori_loop(0, chips, arrived, 0)
        parts = [rx.at[s] for s in range(chips)]
        slot = 0
        while len(parts) > 1:
            pairs = list(zip(parts[::2], parts[1::2]))
            results = [joined(late[...], early[...]) for early, late in pairs]
            fresh = []
            for result in results:
                tree[slot] = result
                fresh.append(tree.at[slot])
                slot += 1
            parts = fresh + (parts[-1:] if len(parts) % 2 else [])

        @pl.when(seg == 0)
        def _():
            first_state[...] = applied(tree[chips - 2], init_ref[...])
            for g in range(segs - 1, 0, -1):
                fput(g).start()

        for g in range(segs - 1, 1, -1):

            @pl.when((seg > 0) & (seg < g))
            def _():
                zput(g).start()

        total[:, :dk] = jnp.where(iota((dk, dk), 0) == iota((dk, dk), 1), 1.0, 0.0).astype(F32)
        total[:, dk:] = jnp.zeros((dk, dv), F32)

        def one(s, _):
            so_far = total[...]
            prefix[s] = so_far
            total[...] = joined(rx[s], so_far)
            return 0

        lax.fori_loop(0, chips, one, 0)

        @pl.when(seg == 0)
        def _():
            state[...] = init_ref[...]

        @pl.when(seg > 0)
        def _():
            fput(0).wait_recv()
            state[...] = zstate[...]

        for g in range(1, segs - 1):

            @pl.when(g < seg)
            def _():
                zgot(g).wait_recv()
                state[...] = applied(zx[g], state[...])

        def give(k, _):
            s = lax.rem(2 * chips - 1 - chip + k, chips)
            ready = applied(prefix[s], state[...])

            @pl.when(s != chip)
            def _():
                outgoing[s] = ready
                sput(s, 0).start()

            @pl.when(near(s, chip))
            def _():
                sput(s, 1).start()

            @pl.when(s == chip)
            def _():
                own_state[mine] = ready

            return 0

        lax.fori_loop(0, chips, give, 0)

    def sent(c):
        for h in range(heads):
            mput(h, c).wait_send()

    for_core(sent)

    for h in range(heads):

        @pl.when(me != h * span)
        def _():
            put(h).wait_send()

    @pl.when(owner)
    def _():
        @pl.when(seg == 0)
        def _():
            for g in range(1, segs):
                fput(g).wait_send()

        for g in range(2, segs):

            @pl.when((seg > 0) & (seg < g))
            def _():
                zput(g).wait_send()

    def ordered(k):
        return lax.rem(mine + (k // per) + (k % per) * (heads // per), heads)

    @pl.when(core == 0)
    def _():
        for k in range(heads):
            h = ordered(k)

            @pl.when(me != h * span)
            def _():
                sgot(h).wait_recv()

            @pl.when(relayed(h))
            def _():
                rput(h).start()

    def closing(i, _):
        group = [ordered(i * 2 + d) for d in range(2)]

        @pl.when(core > 0)
        def _():
            for h in group:

                @pl.when(relayed(h))
                def _():
                    rput(h).wait_recv()

                @pl.when(jnp.logical_not(relayed(h)))
                def _():
                    sgot(h).wait_recv()

        states = [split(own_state[h]) for h in group]
        reads = [
            dot(reach[h], jnp.concatenate([hi, hi], 0)) + dot(reach[h, :, :dk], lo) + base[h]
            for h, (hi, lo) in zip(group, states)
        ]
        squares = [jnp.mean(read * read, axis=-1, keepdims=True) for read in reads]
        for h, read, square in zip(group, reads, squares):
            normed = read * lax.rsqrt(square + 1e-6) * gain_ref[pl.ds(h, 1), :]
            qf[pl.ds(h, read.shape[0], stride=heads), :] = normed
        return 0

    lax.fori_loop(0, heads // 2, closing, 0)
    out_ref[...] = qf[...].astype(BF16)

    for h in range(heads):

        @pl.when((core == 0) & relayed(h))
        def _():
            rput(h).wait_send()

    @pl.when(owner)
    def _():
        def done(s, _):
            @pl.when(s != chip)
            def _():
                sput(s, 0).wait_send()

            @pl.when(near(s, chip))
            def _():
                sput(s, 1).wait_send()

            return 0

        lax.fori_loop(0, chips, done, 0)


def per_device(seqs, segs, query_rows, key_rows, value_rows, out_gain, initial_state):
    _, tokens, heads, dk = query_rows.shape
    dv = value_rows.shape[-1]
    steps = tokens * REFL
    nblk = steps // BLK
    per = 2
    count = heads * nblk
    wide = dk + dv
    chips = seqs // CORES
    anywhere = pl.BlockSpec(memory_space=pl.ANY)
    vmem = pl.BlockSpec(memory_space=pltpu.VMEM)
    dma = pltpu.SemaphoreType.DMA
    out = pl.pallas_call(
        functools.partial(kernel, seqs, segs, heads, per),
        in_specs=[anywhere] * 5,
        out_specs=vmem,
        out_shape=pltpu.VMEM((tokens * heads, dv), BF16),
        scratch_shapes=[
            pltpu.VMEM((tokens * heads, dk), BF16),
            pltpu.VMEM((steps * heads, dk), BF16),
            pltpu.VMEM((steps * heads, dv), BF16),
            pltpu.VMEM((heads, dv), F32),
            pltpu.VMEM((dk, dv), F32),
            dma((5,)),
            pltpu.VMEM((tokens * heads, dk), F32),
            pltpu.VMEM((steps * heads, dk), F32),
            pltpu.VMEM((steps * heads, dv), F32),
            pltpu.VMEM((count * SUB, BLK), F32),
            pltpu.VMEM((count * SUB, BLK), F32),
            pltpu.VMEM((count, BLK, BLK), F32),
            pltpu.VMEM((count, 1, BLK), F32),
            pltpu.VMEM((heads, nblk, BLK, dk), BF16),
            pltpu.VMEM((heads, nblk, dk, wide), F32),
            pltpu.VMEM((heads, nblk, BLK, wide), BF16),
            pltpu.VMEM((heads, nblk, BLK, wide), BF16),
            pltpu.VMEM((heads, nblk, dk, wide), F32),
            pltpu.VMEM((CORES, heads, dk, wide), F32),
            pltpu.VMEM((heads, dk // CORES, wide), F32),
            pltpu.VMEM((heads, tokens, 2 * dk), BF16),
            pltpu.VMEM((heads, tokens, dv), F32),
            pltpu.VMEM((chips, dk, wide), F32),
            pltpu.VMEM((chips, dk, wide), F32),
            pltpu.VMEM((chips, dk, dv), F32),
            pltpu.VMEM((dk, wide), F32),
            pltpu.VMEM((chips - 1, dk, wide), F32),
            pltpu.VMEM((segs, dk, wide), F32),
            pltpu.VMEM((dk, dv), F32),
            pltpu.VMEM((dk, dv), F32),
            pltpu.VMEM((heads, dk, dv), F32),
            pltpu.VMEM((dk, dv), F32),
            dma((heads,)),
            dma((heads,)),
            dma((heads,)),
            dma((chips, CORES)),
            dma((segs,)),
            dma((segs,)),
            dma((chips, CORES)),
            dma((heads,)),
            dma((heads,)),
            dma((heads,)),
        ],
        compiler_params=pltpu.CompilerParams(collective_id=0, has_side_effects=True),
        name="delta_product",
    )(
        query_rows.reshape(tokens * heads, dk),
        key_rows.reshape(steps * heads, dk),
        value_rows.reshape(steps * heads, dv),
        out_gain,
        initial_state,
    )
    return out.reshape(1, tokens, heads, dv)


def solution(mesh):
    return jax.shard_map(
        functools.partial(per_device, mesh.shape["seq"], mesh.shape["seg"]),
        mesh=mesh,
        in_specs=(
            P("seg", "seq", None, None),
            P("seg", "seq", None, None, None),
            P("seg", "seq", None, None, None),
            P(),
            P(),
        ),
        out_specs=P("seg", "seq", None, None),
        check_vma=False,
    )
```

```python
import functools

import jax
import jax.numpy as jnp
from jax import lax
from jax.experimental import pallas as pl
from jax.experimental.pallas import tpu as pltpu
from jax.sharding import PartitionSpec as P

F32 = jnp.float32
BF16 = jnp.bfloat16
REFL = 2
CORES = 2
BLK = 128
SUB = 16
LANES = 128
MESH = pl.DeviceIdType.MESH


def dot(a, b):
    return lax.dot_general(a, b, (((1,), (0,)), ((), ())), preferred_element_type=F32)


def dot_bt(a, b):
    return lax.dot_general(a, b, (((1,), (1,)), ((), ())), preferred_element_type=F32)


def dot_at(a, b):
    return lax.dot_general(a, b, (((0,), (0,)), ((), ())), preferred_element_type=F32)


def split(x):
    high = x.astype(BF16)
    return high, (x - high.astype(F32)).astype(BF16)


def dot3(a, b):
    ah, al = a
    bh, bl = b
    rows, width = ah.shape[0], bh.shape[1]
    both = jnp.concatenate([ah, al], 0)
    if width <= LANES:
        full = dot(both, jnp.concatenate([bh, bl], 1))
        return full[:rows, :width] + (full[:rows, width:] + full[rows:, :width])
    full = dot(both, bh)
    return full[:rows] + (full[rows:] + dot(ah, bl))


def dot2(a, exact):
    rows = a[0].shape[0]
    full = dot(jnp.concatenate(a, 0), exact)
    return full[:rows] + full[rows:]


def iota(shape, axis):
    return lax.broadcasted_iota(jnp.int32, shape, axis)


def grouped(x, size, odd):
    return [x[g * size : (g + 1) * size] for g in range(odd, x.shape[0] // size, 2)]


def joined(late, early):
    dk = early.shape[0]
    after = compose(late[:, :dk], early)
    return jnp.concatenate([after[:, :dk], after[:, dk:] + late[:, dk:]], axis=1)


def invert_level(inv, low, size):
    half = BLK // 2
    paired = iota((half, BLK), 1) // size == 2 * (iota((half, BLK), 0) // size)
    high, rest = split(inv)
    under = jnp.where(paired, jnp.concatenate(grouped(low, size, 1), 0), 0.0)
    if 2 * size == BLK:
        part = dot3(split(under[:, :size]), (high[:size], rest[:size]))
    else:
        part = dot3(split(under), (high, rest))
    blank = jnp.zeros((size, BLK), F32)
    spread = []
    for g in range(half // size):
        spread += [blank, part[g * size : (g + 1) * size]]
    own = tuple(jnp.concatenate(grouped(x, size, 1), 0) for x in (high, rest))
    fill = dot3(own, split(jnp.concatenate(spread, 0)))
    even, odd = grouped(inv, size, 0), grouped(inv, size, 1)
    rows = []
    for g in range(half // size):
        rows += [even[g], odd[g] - fill[g * size : (g + 1) * size]]
    return jnp.concatenate(rows, 0)


def wide(x):
    return jnp.concatenate(split(x), 1)


def tall(x):
    return jnp.concatenate(split(x), 0)


def compose_split(left, right):
    lh, ll = left
    rh, rl = right
    return dot(jnp.concatenate([lh, ll], 1), jnp.concatenate([rh, rh], 0)) + dot(lh, rl)


def compose(left, right):
    return compose_split(split(left), split(right))


def grams(first, per, heads, nblk, kf, dsc, low, norm, kb):
    row, col = iota((BLK, BLK), 0), iota((BLK, BLK), 1)
    eye = row == col
    lane = iota((SUB, BLK), 1)
    at = [(first + n // nblk, n % nblk) for n in range(per * nblk)]
    products, squares = [], []
    for n, (h, c) in enumerate(at):
        key = kf[pl.ds(c * BLK * heads + h, BLK, stride=heads), :].astype(BF16)
        kb[h, c] = key
        products.append(dot_bt(key, key))
        yield
    for n, gram in enumerate(products):
        diag = jnp.where(eye, gram, 0.0)
        squares.append(jnp.sum(diag, axis=1, keepdims=True))
        norm[first * nblk + n] = lax.rsqrt(jnp.sum(diag, axis=0, keepdims=True) + 1e-6)
        yield
    for n, gram in enumerate(products):
        rcol = lax.rsqrt(squares[n] + 1e-6)
        lower = jnp.where(row > col, gram * (2.0 * rcol * rcol), 0.0)
        low[first * nblk + n] = lower
        packed = lower[:SUB]
        for g in range(1, BLK // SUB):
            packed = jnp.where(lane // SUB == g, lower[g * SUB : (g + 1) * SUB], packed)
        dsc[pl.ds(pl.multiple_of((first * nblk + n) * SUB, SUB), SUB), :] = packed
        yield


def substitute(first, count, dsc, nsc):
    lane = iota((count, BLK), 1)
    solved = []
    for i in range(SUB):
        line = dsc[pl.ds(first * SUB + i, count, stride=SUB), :]
        total = jnp.where(lane % SUB == i, 1.0, 0.0)
        for j in range(i):
            factor = jnp.take_along_axis(line, (lane // SUB) * SUB + j, axis=1)
            total = total - factor * solved[j]
        solved.append(total)
        nsc[pl.ds(first * SUB + i, count, stride=SUB), :] = total
        yield


def factors(beside, first, per, heads, nblk, vf, nsc, low, norm, kb, steps, scaled_hi, scaled_lo, before, both, core):
    dk = kb.shape[-1]
    eye = iota((BLK, BLK), 0) == iota((BLK, BLK), 1)
    lane = iota((SUB, BLK), 1)
    inverses = []
    base = first * nblk
    for n in range(per * nblk):
        packed = nsc[pl.ds(pl.multiple_of((base + n) * SUB, SUB), SUB), :]
        inverses.append(
            jnp.concatenate(
                [jnp.where(lane // SUB == g, packed, 0.0) for g in range(BLK // SUB)], axis=0
            )
        )
    size = SUB
    while size < BLK:
        for n in range(per * nblk):
            inverses[n] = invert_level(inverses[n], low[base + n], size)
            for _ in range(2):
                next(beside, None)
        size *= 2
    for _ in beside:
        pass

    count = per * nblk
    at = [(first + n // nblk, n % nblk) for n in range(count)]
    keys = [kb[h, c] for h, c in at]
    keys = [jnp.concatenate([key, key], 0) for key in keys]
    values = [vf[pl.ds(c * BLK * heads + h, BLK, stride=heads), :].astype(BF16) for h, c in at]
    rrows = [norm[base + n] for n in range(count)]
    doubled = [inv * (2.0 * rrow) for inv, rrow in zip(inverses, rrows)]
    updates = [dot(wide(d), jnp.concatenate([v, v], 0)) for d, v in zip(doubled, values)]
    weights = [dot(wide(d * rrow), key) for d, rrow, key in zip(doubled, rrows, keys)]
    scaled = [split(jnp.concatenate([w, u], axis=1)) for w, u in zip(weights, updates)]
    moved = [dot_at(key, jnp.concatenate(s, 0)) for key, s in zip(keys, scaled)]
    for (h, c), s in zip(at, scaled):
        scaled_hi[h, c] = s[0]
        scaled_lo[h, c] = s[1]
    unit = jnp.where(eye, 1.0, 0.0)
    nodes = [jnp.concatenate([unit - m[:, :dk], m[:, dk:]], axis=1) for m in moved]
    for n, (h, c) in enumerate(at):
        if c & (c + 1):
            steps[h, c] = nodes[n]
    nodes = [nodes[h * nblk : (h + 1) * nblk] for h in range(per)]
    reached = 1
    while len(nodes[0]) > 1:
        for h in range(per):
            before[first + h, reached] = nodes[h][0]
        nodes = [[joined(late, early) for early, late in zip(x[::2], x[1::2])] for x in nodes]
        reached *= 2
    for h in range(per):
        both[core, first + h] = nodes[h][0]


def readers(h, heads, nblk, qf, kb, steps, scaled_hi, scaled_lo, before, reach, base):
    dk = qf.shape[1]
    tok = BLK // REFL
    visible = iota((tok, BLK), 1) <= REFL * iota((tok, BLK), 0) + (REFL - 1)
    blocks = range(nblk)
    queries = [qf[pl.ds(c * tok * heads + h, tok, stride=heads), :] for c in blocks]
    scores = [dot_bt(queries[c].astype(BF16), kb[h, c]) for c in blocks]
    scores = [split(jnp.where(visible, score, 0.0)) for score in scores]
    reads = [compose_split(scores[c], (scaled_hi[h, c], scaled_lo[h, c])) for c in blocks]
    gone = [split(query - read[:, :dk]) for query, read in zip(queries, reads)]
    reach[h, :tok, :] = jnp.concatenate(gone[0], 1)
    base[h, :tok, :] = reads[0][:, dk:]
    so_far = None
    for c in range(1, nblk):
        rows = slice(c * tok, (c + 1) * tok)
        so_far = joined(steps[h, c - 1], so_far) if c & (c - 1) else before[h, c]
        moved = compose_split(gone[c], split(so_far))
        reach[h, rows, :] = wide(moved[:, :dk])
        base[h, rows, :] = moved[:, dk:] + reads[c][:, dk:]


def applied(step, state):
    dk = step.shape[0]
    return compose(step[:, :dk], state) + step[:, dk:]


def folding(h, both, reach, base):
    dk = both.shape[2]
    moved = compose_split((reach[h, :, :dk], reach[h, :, dk:]), split(both[0, h]))
    reach[h] = wide(moved[:, :dk])
    base[h] = base[h] + moved[:, dk:]


def kernel(
    seqs, segs, heads, per,
    q_any, k_any, v_any, gain_any, init_any, out_ref,
    q_ref, k_ref, v_ref, gain_ref, init_ref, in_sem,
    qf, kf, vf, dsc, nsc, low, norm, kb, steps, scaled_hi, scaled_lo, before, both, merged, reach, base,
    rx, prefix, outgoing, total, tree, zx, first_state, zstate, own_state, state,
    mput_sem, mgot_sem, put_sem, got_sem, zput_sem, zgot_sem, sput_sem, sgot_sem, rput_sem, rgot_sem,
):
    dk = init_ref.shape[0]
    dv = init_ref.shape[1]
    half = dk // CORES
    nblk = k_ref.shape[0] // (heads * BLK)
    span = seqs // heads
    chips = seqs // CORES
    me = lax.axis_index("seq")
    seg = lax.axis_index("seg")
    core = lax.rem(me, CORES)
    chip = me // CORES
    mate = me + 1 - 2 * core
    owner = lax.rem(me, span) == 0
    mine = me // span
    mine_rows = pl.ds(pl.multiple_of(core * half, half), half)

    def near(first, second):
        return (first != second) & ((first // 2 == second // 2) | (first % 2 == second % 2))

    def relayed(h):
        return jnp.logical_not(near(h * span // CORES, chip))

    loads = [
        pltpu.make_async_copy(src, dst, in_sem.at[i])
        for i, (src, dst) in enumerate(
            [
                (k_any, k_ref),
                (v_any, v_ref),
                (q_any, q_ref),
                (gain_any, gain_ref),
                (init_any.at[mine], init_ref),
            ]
        )
    ]
    for load in loads:
        load.start()
    barrier = pltpu.get_barrier_semaphore()
    for d in range(1, seqs):
        pl.semaphore_signal(
            barrier, inc=1,
            device_id={"seq": lax.rem(me + d, seqs), "seg": seg}, device_id_type=MESH,
        )
    for d in range(1, segs):
        pl.semaphore_signal(
            barrier, inc=1,
            device_id={"seq": me, "seg": lax.rem(seg + d, segs)}, device_id_type=MESH,
        )

    def copy(src, dst, put, got, to_seq, to_seg):
        return pltpu.make_async_remote_copy(
            src_ref=src, dst_ref=dst, send_sem=put, recv_sem=got,
            device_id={"seq": to_seq, "seg": to_seg}, device_id_type=MESH,
        )

    def mput(h, c):
        ref = both.at[c, h] if c == 0 else both.at[c, h, :half]
        return copy(ref, ref, mput_sem.at[h], mgot_sem.at[h], mate, seg)

    def for_core(action):
        for c in range(CORES):

            @pl.when(core == c)
            def _():
                action(c)

    def put(h):
        return copy(
            merged.at[h], rx.at[chip, mine_rows], put_sem.at[h], got_sem.at[chip, core], h * span, seg
        )

    def got(s, c):
        ref = rx.at[s, pl.ds(c * half, half)]
        return copy(ref, ref, put_sem.at[0], got_sem.at[s, c], s * CORES, seg)

    def sput(s, c):
        return copy(
            outgoing.at[s], own_state.at[mine], sput_sem.at[s, c], sgot_sem.at[mine], s * CORES + c, seg
        )

    def sgot(h):
        return copy(own_state.at[h], own_state.at[h], sput_sem.at[0, 0], sgot_sem.at[h], h * span, seg)

    def rput(h):
        return copy(own_state.at[h], own_state.at[h], rput_sem.at[h], rgot_sem.at[h], mate, seg)

    def zput(g):
        return copy(tree.at[chips - 2], zx.at[seg], zput_sem.at[g], zgot_sem.at[seg], me, g)

    def zgot(g):
        return copy(tree.at[chips - 2], zx.at[g], zput_sem.at[g], zgot_sem.at[g], me, g)

    def fput(g):
        return copy(first_state, zstate, zput_sem.at[g], zgot_sem.at[0], me, g)

    loads[0].wait()
    kf[...] = k_ref[...].astype(F32)

    def group_of(i):
        turn = lax.rem(i + 1 + mine // per, heads // per)
        return turn, [turn * per + lax.rem(mine + 1 + d, per) for d in range(per)]

    def prepared(first):
        yield from grams(first, per, heads, nblk, kf, dsc, low, norm, kb)
        yield from substitute(first * nblk, per * nblk, dsc, nsc)

    for _ in prepared(group_of(0)[0] * per):
        pass

    for load in loads[1:]:
        load.wait()
    vf[...] = v_ref[...].astype(F32)

    def local(i, _):
        turn, group = group_of(i)
        @pl.when(i + 1 < heads // per)
        def _():
            beside = prepared(group_of(i + 1)[0] * per)
            factors(beside, turn * per, per, heads, nblk, vf, nsc, low, norm, kb, steps, scaled_hi, scaled_lo, before, both, core)

        @pl.when(i + 1 == heads // per)
        def _():
            beside = iter(())
            factors(beside, turn * per, per, heads, nblk, vf, nsc, low, norm, kb, steps, scaled_hi, scaled_lo, before, both, core)

        @pl.when(i == 0)
        def _():
            pl.semaphore_wait(barrier, seqs + segs - 2)

        def exchange(c):
            for h in group:
                mput(h, c).start()

        for_core(exchange)
        return 0

    lax.fori_loop(0, heads // per, local, 0)

    def merging(group):
        def arrived(c):
            for h in group:
                mput(h, 1 - c).wait_recv()

        for_core(arrived)
        results = [joined(both[1, h, mine_rows], both[0, h]) for h in group]
        for h, result in zip(group, results):
            merged[h] = result

            @pl.when(me != h * span)
            def _():
                put(h).start()

            @pl.when(me == h * span)
            def _():
                rx[chip, mine_rows] = merged[h]

    def merging_all(i, _):
        merging(group_of(i)[1])
        return 0

    lax.fori_loop(0, heads // per - 1, merging_all, 0)

    def merging_one(d, _):
        merging([group_of(heads // per - 1)[0] * per + lax.rem(mine + 1 + d, per)])
        return 0

    lax.fori_loop(0, per, merging_one, 0)

    qf[...] = q_ref[...].astype(F32)

    def reading(h, _):
        readers(h, heads, nblk, qf, kb, steps, scaled_hi, scaled_lo, before, reach, base)
        return 0

    lax.fori_loop(0, heads, reading, 0)

    @pl.when(core > 0)
    def _():
        def fold(h, _):
            folding(h, both, reach, base)
            return 0

        lax.fori_loop(0, heads, fold, 0)

    @pl.when(owner)
    def _():
        def arrived(s, _):
            for c in range(CORES):

                @pl.when(s * CORES + c != me)
                def _():
                    got(s, c).wait_recv()

            return 0

        lax.fori_loop(0, chips, arrived, 0)
        parts = [rx.at[s] for s in range(chips)]
        slot = 0
        while len(parts) > 1:
            pairs = list(zip(parts[::2], parts[1::2]))
            results = [joined(late[...], early[...]) for early, late in pairs]
            fresh = []
            for result in results:
                tree[slot] = result
                fresh.append(tree.at[slot])
                slot += 1
            parts = fresh + (parts[-1:] if len(parts) % 2 else [])

        @pl.when(seg == 0)
        def _():
            first_state[...] = applied(tree[chips - 2], init_ref[...])
            for g in range(segs - 1, 0, -1):
                fput(g).start()

        for g in range(segs - 1, 1, -1):

            @pl.when((seg > 0) & (seg < g))
            def _():
                zput(g).start()

        total[:, :dk] = jnp.where(iota((dk, dk), 0) == iota((dk, dk), 1), 1.0, 0.0).astype(F32)
        total[:, dk:] = jnp.zeros((dk, dv), F32)

        def one(s, _):
            so_far = total[...]
            prefix[s] = so_far
            total[...] = joined(rx[s], so_far)
            return 0

        lax.fori_loop(0, chips, one, 0)

        @pl.when(seg == 0)
        def _():
            state[...] = init_ref[...]

        @pl.when(seg > 0)
        def _():
            fput(0).wait_recv()
            state[...] = zstate[...]

        for g in range(1, segs - 1):

            @pl.when(g < seg)
            def _():
                zgot(g).wait_recv()
                state[...] = applied(zx[g], state[...])

        def give(k, _):
            s = lax.rem(2 * chips - 1 - chip + k, chips)
            ready = applied(prefix[s], state[...])

            @pl.when(s != chip)
            def _():
                outgoing[s] = ready
                sput(s, 0).start()

            @pl.when(near(s, chip))
            def _():
                sput(s, 1).start()

            @pl.when(s == chip)
            def _():
                own_state[mine] = ready

            return 0

        lax.fori_loop(0, chips, give, 0)

    def sent(c):
        for h in range(heads):
            mput(h, c).wait_send()

    for_core(sent)

    for h in range(heads):

        @pl.when(me != h * span)
        def _():
            put(h).wait_send()

    @pl.when(owner)
    def _():
        @pl.when(seg == 0)
        def _():
            for g in range(1, segs):
                fput(g).wait_send()

        for g in range(2, segs):

            @pl.when((seg > 0) & (seg < g))
            def _():
                zput(g).wait_send()

    def ordered(k):
        return lax.rem(mine + (k // per) + (k % per) * (heads // per), heads)

    @pl.when(core == 0)
    def _():
        for k in range(heads):
            h = ordered(k)

            @pl.when(me != h * span)
            def _():
                sgot(h).wait_recv()

            @pl.when(relayed(h))
            def _():
                rput(h).start()

    def closing(i, _):
        group = [ordered(i * 2 + d) for d in range(2)]

        @pl.when(core > 0)
        def _():
            for h in group:

                @pl.when(relayed(h))
                def _():
                    rput(h).wait_recv()

                @pl.when(jnp.logical_not(relayed(h)))
                def _():
                    sgot(h).wait_recv()

        states = [split(own_state[h]) for h in group]
        reads = [
            dot(reach[h], jnp.concatenate([hi, hi], 0)) + dot(reach[h, :, :dk], lo) + base[h]
            for h, (hi, lo) in zip(group, states)
        ]
        squares = [jnp.mean(read * read, axis=-1, keepdims=True) for read in reads]
        for h, read, square in zip(group, reads, squares):
            normed = read * lax.rsqrt(square + 1e-6) * gain_ref[pl.ds(h, 1), :]
            qf[pl.ds(h, read.shape[0], stride=heads), :] = normed
        return 0

    lax.fori_loop(0, heads // 2, closing, 0)
    out_ref[...] = qf[...].astype(BF16)

    for h in range(heads):

        @pl.when((core == 0) & relayed(h))
        def _():
            rput(h).wait_send()

    @pl.when(owner)
    def _():
        def done(s, _):
            @pl.when(s != chip)
            def _():
                sput(s, 0).wait_send()

            @pl.when(near(s, chip))
            def _():
                sput(s, 1).wait_send()

            return 0

        lax.fori_loop(0, chips, done, 0)


def per_device(seqs, segs, query_rows, key_rows, value_rows, out_gain, initial_state):
    _, tokens, heads, dk = query_rows.shape
    dv = value_rows.shape[-1]
    steps = tokens * REFL
    nblk = steps // BLK
    per = 2
    count = heads * nblk
    wide = dk + dv
    chips = seqs // CORES
    anywhere = pl.BlockSpec(memory_space=pl.ANY)
    vmem = pl.BlockSpec(memory_space=pltpu.VMEM)
    dma = pltpu.SemaphoreType.DMA
    out = pl.pallas_call(
        functools.partial(kernel, seqs, segs, heads, per),
        in_specs=[anywhere] * 5,
        out_specs=vmem,
        out_shape=pltpu.VMEM((tokens * heads, dv), BF16),
        scratch_shapes=[
            pltpu.VMEM((tokens * heads, dk), BF16),
            pltpu.VMEM((steps * heads, dk), BF16),
            pltpu.VMEM((steps * heads, dv), BF16),
            pltpu.VMEM((heads, dv), F32),
            pltpu.VMEM((dk, dv), F32),
            dma((5,)),
            pltpu.VMEM((tokens * heads, dk), F32),
            pltpu.VMEM((steps * heads, dk), F32),
            pltpu.VMEM((steps * heads, dv), F32),
            pltpu.VMEM((count * SUB, BLK), F32),
            pltpu.VMEM((count * SUB, BLK), F32),
            pltpu.VMEM((count, BLK, BLK), F32),
            pltpu.VMEM((count, 1, BLK), F32),
            pltpu.VMEM((heads, nblk, BLK, dk), BF16),
            pltpu.VMEM((heads, nblk, dk, wide), F32),
            pltpu.VMEM((heads, nblk, BLK, wide), BF16),
            pltpu.VMEM((heads, nblk, BLK, wide), BF16),
            pltpu.VMEM((heads, nblk, dk, wide), F32),
            pltpu.VMEM((CORES, heads, dk, wide), F32),
            pltpu.VMEM((heads, dk // CORES, wide), F32),
            pltpu.VMEM((heads, tokens, 2 * dk), BF16),
            pltpu.VMEM((heads, tokens, dv), F32),
            pltpu.VMEM((chips, dk, wide), F32),
            pltpu.VMEM((chips, dk, wide), F32),
            pltpu.VMEM((chips, dk, dv), F32),
            pltpu.VMEM((dk, wide), F32),
            pltpu.VMEM((chips - 1, dk, wide), F32),
            pltpu.VMEM((segs, dk, wide), F32),
            pltpu.VMEM((dk, dv), F32),
            pltpu.VMEM((dk, dv), F32),
            pltpu.VMEM((heads, dk, dv), F32),
            pltpu.VMEM((dk, dv), F32),
            dma((heads,)),
            dma((heads,)),
            dma((heads,)),
            dma((chips, CORES)),
            dma((segs,)),
            dma((segs,)),
            dma((chips, CORES)),
            dma((heads,)),
            dma((heads,)),
            dma((heads,)),
        ],
        compiler_params=pltpu.CompilerParams(collective_id=0, has_side_effects=True),
        name="delta_product",
    )(
        query_rows.reshape(tokens * heads, dk),
        key_rows.reshape(steps * heads, dk),
        value_rows.reshape(steps * heads, dv),
        out_gain,
        initial_state,
    )
    return out.reshape(1, tokens, heads, dv)


def solution(mesh):
    return jax.shard_map(
        functools.partial(per_device, mesh.shape["seq"], mesh.shape["seg"]),
        mesh=mesh,
        in_specs=(
            P("seg", "seq", None, None),
            P("seg", "seq", None, None, None),
            P("seg", "seq", None, None, None),
            P(),
            P(),
        ),
        out_specs=P("seg", "seq", None, None),
        check_vma=False,
    )
```

```python
import functools

import jax
import jax.numpy as jnp
from jax import lax
from jax.experimental import pallas as pl
from jax.experimental.pallas import tpu as pltpu
from jax.sharding import PartitionSpec as P

F32 = jnp.float32
BF16 = jnp.bfloat16
REFL = 2
CORES = 2
BLK = 128
SUB = 16
LANES = 128
MESH = pl.DeviceIdType.MESH


def dot(a, b):
    return lax.dot_general(a, b, (((1,), (0,)), ((), ())), preferred_element_type=F32)


def dot_bt(a, b):
    return lax.dot_general(a, b, (((1,), (1,)), ((), ())), preferred_element_type=F32)


def dot_at(a, b):
    return lax.dot_general(a, b, (((0,), (0,)), ((), ())), preferred_element_type=F32)


def split(x):
    high = x.astype(BF16)
    return high, (x - high.astype(F32)).astype(BF16)


def dot3(a, b):
    ah, al = a
    bh, bl = b
    rows, width = ah.shape[0], bh.shape[1]
    both = jnp.concatenate([ah, al], 0)
    if width <= LANES:
        full = dot(both, jnp.concatenate([bh, bl], 1))
        return full[:rows, :width] + (full[:rows, width:] + full[rows:, :width])
    full = dot(both, bh)
    return full[:rows] + (full[rows:] + dot(ah, bl))


def dot2(a, exact):
    rows = a[0].shape[0]
    full = dot(jnp.concatenate(a, 0), exact)
    return full[:rows] + full[rows:]


def iota(shape, axis):
    return lax.broadcasted_iota(jnp.int32, shape, axis)


def grouped(x, size, odd):
    return [x[g * size : (g + 1) * size] for g in range(odd, x.shape[0] // size, 2)]


def joined(late, early):
    dk = early.shape[0]
    after = compose(late[:, :dk], early)
    return jnp.concatenate([after[:, :dk], after[:, dk:] + late[:, dk:]], axis=1)


def invert_level(inv, low, size):
    half = BLK // 2
    paired = iota((half, BLK), 1) // size == 2 * (iota((half, BLK), 0) // size)
    high, rest = split(inv)
    under = jnp.where(paired, jnp.concatenate(grouped(low, size, 1), 0), 0.0)
    if 2 * size == BLK:
        part = dot3(split(under[:, :size]), (high[:size], rest[:size]))
    else:
        part = dot3(split(under), (high, rest))
    blank = jnp.zeros((size, BLK), F32)
    spread = []
    for g in range(half // size):
        spread += [blank, part[g * size : (g + 1) * size]]
    own = tuple(jnp.concatenate(grouped(x, size, 1), 0) for x in (high, rest))
    fill = dot3(own, split(jnp.concatenate(spread, 0)))
    even, odd = grouped(inv, size, 0), grouped(inv, size, 1)
    rows = []
    for g in range(half // size):
        rows += [even[g], odd[g] - fill[g * size : (g + 1) * size]]
    return jnp.concatenate(rows, 0)


def wide(x):
    return jnp.concatenate(split(x), 1)


def tall(x):
    return jnp.concatenate(split(x), 0)


def compose_split(left, right):
    lh, ll = left
    rh, rl = right
    return dot(jnp.concatenate([lh, ll], 1), jnp.concatenate([rh, rh], 0)) + dot(lh, rl)


def compose(left, right):
    return compose_split(split(left), split(right))


def grams(first, per, heads, nblk, kf, dsc, low, norm, kb):
    row, col = iota((BLK, BLK), 0), iota((BLK, BLK), 1)
    eye = row == col
    lane = iota((SUB, BLK), 1)
    at = [(first + n // nblk, n % nblk) for n in range(per * nblk)]
    products, squares = [], []
    for n, (h, c) in enumerate(at):
        key = kf[pl.ds(c * BLK * heads + h, BLK, stride=heads), :].astype(BF16)
        kb[h, c] = key
        products.append(dot_bt(key, key))
        yield
    for n, gram in enumerate(products):
        diag = jnp.where(eye, gram, 0.0)
        squares.append(jnp.sum(diag, axis=1, keepdims=True))
        norm[first * nblk + n] = lax.rsqrt(jnp.sum(diag, axis=0, keepdims=True) + 1e-6)
        yield
    for n, gram in enumerate(products):
        rcol = lax.rsqrt(squares[n] + 1e-6)
        lower = jnp.where(row > col, gram * (2.0 * rcol * rcol), 0.0)
        low[first * nblk + n] = lower
        packed = lower[:SUB]
        for g in range(1, BLK // SUB):
            packed = jnp.where(lane // SUB == g, lower[g * SUB : (g + 1) * SUB], packed)
        dsc[pl.ds(pl.multiple_of((first * nblk + n) * SUB, SUB), SUB), :] = packed
        yield


def substitute(first, count, dsc, nsc):
    lane = iota((count, BLK), 1)
    solved = []
    for i in range(SUB):
        line = dsc[pl.ds(first * SUB + i, count, stride=SUB), :]
        total = jnp.where(lane % SUB == i, 1.0, 0.0)
        for j in range(i):
            factor = jnp.take_along_axis(line, (lane // SUB) * SUB + j, axis=1)
            total = total - factor * solved[j]
        solved.append(total)
        nsc[pl.ds(first * SUB + i, count, stride=SUB), :] = total
        yield


def factors(beside, first, per, heads, nblk, vf, nsc, low, norm, kb, steps, scaled_hi, scaled_lo, before, both, core):
    dk = kb.shape[-1]
    eye = iota((BLK, BLK), 0) == iota((BLK, BLK), 1)
    lane = iota((SUB, BLK), 1)
    inverses = []
    base = first * nblk
    for n in range(per * nblk):
        packed = nsc[pl.ds(pl.multiple_of((base + n) * SUB, SUB), SUB), :]
        inverses.append(
            jnp.concatenate(
                [jnp.where(lane // SUB == g, packed, 0.0) for g in range(BLK // SUB)], axis=0
            )
        )
    size = SUB
    while size < BLK:
        for n in range(per * nblk):
            inverses[n] = invert_level(inverses[n], low[base + n], size)
            for _ in range(2):
                next(beside, None)
        size *= 2
    for _ in beside:
        pass

    count = per * nblk
    at = [(first + n // nblk, n % nblk) for n in range(count)]
    keys = [kb[h, c] for h, c in at]
    keys = [jnp.concatenate([key, key], 0) for key in keys]
    values = [vf[pl.ds(c * BLK * heads + h, BLK, stride=heads), :].astype(BF16) for h, c in at]
    rrows = [norm[base + n] for n in range(count)]
    doubled = [inv * (2.0 * rrow) for inv, rrow in zip(inverses, rrows)]
    updates = [dot(wide(d), jnp.concatenate([v, v], 0)) for d, v in zip(doubled, values)]
    weights = [dot(wide(d * rrow), key) for d, rrow, key in zip(doubled, rrows, keys)]
    scaled = [split(jnp.concatenate([w, u], axis=1)) for w, u in zip(weights, updates)]
    moved = [dot_at(key, jnp.concatenate(s, 0)) for key, s in zip(keys, scaled)]
    for (h, c), s in zip(at, scaled):
        scaled_hi[h, c] = s[0]
        scaled_lo[h, c] = s[1]
    unit = jnp.where(eye, 1.0, 0.0)
    nodes = [jnp.concatenate([unit - m[:, :dk], m[:, dk:]], axis=1) for m in moved]
    for n, (h, c) in enumerate(at):
        if c & (c + 1):
            steps[h, c] = nodes[n]
    nodes = [nodes[h * nblk : (h + 1) * nblk] for h in range(per)]
    reached = 1
    while len(nodes[0]) > 1:
        for h in range(per):
            before[first + h, reached] = nodes[h][0]
        nodes = [[joined(late, early) for early, late in zip(x[::2], x[1::2])] for x in nodes]
        reached *= 2
    for h in range(per):
        both[core, first + h] = nodes[h][0]


def readers(h, heads, nblk, qf, kb, steps, scaled_hi, scaled_lo, before, reach, base):
    dk = qf.shape[1]
    tok = BLK // REFL
    visible = iota((tok, BLK), 1) <= REFL * iota((tok, BLK), 0) + (REFL - 1)
    blocks = range(nblk)
    queries = [qf[pl.ds(c * tok * heads + h, tok, stride=heads), :] for c in blocks]
    scores = [dot_bt(queries[c].astype(BF16), kb[h, c]) for c in blocks]
    scores = [split(jnp.where(visible, score, 0.0)) for score in scores]
    reads = [compose_split(scores[c], (scaled_hi[h, c], scaled_lo[h, c])) for c in blocks]
    gone = [split(query - read[:, :dk]) for query, read in zip(queries, reads)]
    reach[h, :tok, :] = jnp.concatenate(gone[0], 1)
    base[h, :tok, :] = reads[0][:, dk:]
    so_far = None
    for c in range(1, nblk):
        rows = slice(c * tok, (c + 1) * tok)
        so_far = joined(steps[h, c - 1], so_far) if c & (c - 1) else before[h, c]
        moved = compose_split(gone[c], split(so_far))
        reach[h, rows, :] = wide(moved[:, :dk])
        base[h, rows, :] = moved[:, dk:] + reads[c][:, dk:]


def applied(step, state):
    dk = step.shape[0]
    return compose(step[:, :dk], state) + step[:, dk:]


def folding(h, both, reach, base):
    dk = both.shape[2]
    moved = compose_split((reach[h, :, :dk], reach[h, :, dk:]), split(both[0, h]))
    reach[h] = wide(moved[:, :dk])
    base[h] = base[h] + moved[:, dk:]


def kernel(
    seqs, segs, heads, per,
    q_any, k_any, v_any, gain_any, init_any, out_ref,
    q_ref, k_ref, v_ref, gain_ref, init_ref, in_sem,
    qf, kf, vf, dsc, nsc, low, norm, kb, steps, scaled_hi, scaled_lo, before, both, merged, reach, base,
    rx, prefix, outgoing, total, tree, zx, first_state, zstate, own_state, state,
    mput_sem, mgot_sem, put_sem, got_sem, zput_sem, zgot_sem, sput_sem, sgot_sem, rput_sem, rgot_sem,
):
    dk = init_ref.shape[0]
    dv = init_ref.shape[1]
    half = dk // CORES
    nblk = k_ref.shape[0] // (heads * BLK)
    span = seqs // heads
    chips = seqs // CORES
    me = lax.axis_index("seq")
    seg = lax.axis_index("seg")
    core = lax.rem(me, CORES)
    chip = me // CORES
    mate = me + 1 - 2 * core
    owner = lax.rem(me, span) == 0
    mine = me // span
    mine_rows = pl.ds(pl.multiple_of(core * half, half), half)

    def near(first, second):
        return (first != second) & ((first // 2 == second // 2) | (first % 2 == second % 2))

    def relayed(h):
        return jnp.logical_not(near(h * span // CORES, chip))

    loads = [
        pltpu.make_async_copy(src, dst, in_sem.at[i])
        for i, (src, dst) in enumerate(
            [
                (k_any, k_ref),
                (v_any, v_ref),
                (q_any, q_ref),
                (gain_any, gain_ref),
                (init_any.at[mine], init_ref),
            ]
        )
    ]
    for load in loads:
        load.start()
    barrier = pltpu.get_barrier_semaphore()
    for d in range(1, seqs):
        pl.semaphore_signal(
            barrier, inc=1,
            device_id={"seq": lax.rem(me + d, seqs), "seg": seg}, device_id_type=MESH,
        )
    for d in range(1, segs):
        pl.semaphore_signal(
            barrier, inc=1,
            device_id={"seq": me, "seg": lax.rem(seg + d, segs)}, device_id_type=MESH,
        )

    def copy(src, dst, put, got, to_seq, to_seg):
        return pltpu.make_async_remote_copy(
            src_ref=src, dst_ref=dst, send_sem=put, recv_sem=got,
            device_id={"seq": to_seq, "seg": to_seg}, device_id_type=MESH,
        )

    def mput(h, c):
        ref = both.at[c, h] if c == 0 else both.at[c, h, :half]
        return copy(ref, ref, mput_sem.at[h], mgot_sem.at[h], mate, seg)

    def for_core(action):
        for c in range(CORES):

            @pl.when(core == c)
            def _():
                action(c)

    def put(h):
        return copy(
            merged.at[h], rx.at[chip, mine_rows], put_sem.at[h], got_sem.at[chip, core], h * span, seg
        )

    def got(s, c):
        ref = rx.at[s, pl.ds(c * half, half)]
        return copy(ref, ref, put_sem.at[0], got_sem.at[s, c], s * CORES, seg)

    def sput(s, c):
        return copy(
            outgoing.at[s], own_state.at[mine], sput_sem.at[s, c], sgot_sem.at[mine], s * CORES + c, seg
        )

    def sgot(h):
        return copy(own_state.at[h], own_state.at[h], sput_sem.at[0, 0], sgot_sem.at[h], h * span, seg)

    def rput(h):
        return copy(own_state.at[h], own_state.at[h], rput_sem.at[h], rgot_sem.at[h], mate, seg)

    def zput(g):
        return copy(tree.at[chips - 2], zx.at[seg], zput_sem.at[g], zgot_sem.at[seg], me, g)

    def zgot(g):
        return copy(tree.at[chips - 2], zx.at[g], zput_sem.at[g], zgot_sem.at[g], me, g)

    def fput(g):
        return copy(first_state, zstate, zput_sem.at[g], zgot_sem.at[0], me, g)

    loads[0].wait()
    kf[...] = k_ref[...].astype(F32)

    def group_of(i):
        turn = lax.rem(i + 1 + mine // per, heads // per)
        return turn, [turn * per + lax.rem(mine + 1 + d, per) for d in range(per)]

    def prepared(first):
        yield from grams(first, per, heads, nblk, kf, dsc, low, norm, kb)
        yield from substitute(first * nblk, per * nblk, dsc, nsc)

    for _ in prepared(group_of(0)[0] * per):
        pass

    for load in loads[1:]:
        load.wait()
    vf[...] = v_ref[...].astype(F32)

    def local(i, _):
        turn, group = group_of(i)
        @pl.when(i + 1 < heads // per)
        def _():
            beside = prepared(group_of(i + 1)[0] * per)
            factors(beside, turn * per, per, heads, nblk, vf, nsc, low, norm, kb, steps, scaled_hi, scaled_lo, before, both, core)

        @pl.when(i + 1 == heads // per)
        def _():
            beside = iter(())
            factors(beside, turn * per, per, heads, nblk, vf, nsc, low, norm, kb, steps, scaled_hi, scaled_lo, before, both, core)

        @pl.when(i == 0)
        def _():
            pl.semaphore_wait(barrier, seqs + segs - 2)

        def exchange(c):
            for h in group:
                mput(h, c).start()

        for_core(exchange)
        return 0

    lax.fori_loop(0, heads // per, local, 0)

    def merging(group):
        def arrived(c):
            for h in group:
                mput(h, 1 - c).wait_recv()

        for_core(arrived)
        results = [joined(both[1, h, mine_rows], both[0, h]) for h in group]
        for h, result in zip(group, results):
            merged[h] = result

            @pl.when(me != h * span)
            def _():
                put(h).start()

            @pl.when(me == h * span)
            def _():
                rx[chip, mine_rows] = merged[h]

    def merging_all(i, _):
        merging(group_of(i)[1])
        return 0

    lax.fori_loop(0, heads // per - 1, merging_all, 0)

    def merging_one(d, _):
        merging([group_of(heads // per - 1)[0] * per + lax.rem(mine + 1 + d, per)])
        return 0

    lax.fori_loop(0, per, merging_one, 0)

    qf[...] = q_ref[...].astype(F32)

    def reading(h, _):
        readers(h, heads, nblk, qf, kb, steps, scaled_hi, scaled_lo, before, reach, base)
        return 0

    lax.fori_loop(0, heads, reading, 0)

    @pl.when(core > 0)
    def _():
        def fold(h, _):
            folding(h, both, reach, base)
            return 0

        lax.fori_loop(0, heads, fold, 0)

    @pl.when(owner)
    def _():
        def arrived(s, _):
            for c in range(CORES):

                @pl.when(s * CORES + c != me)
                def _():
                    got(s, c).wait_recv()

            return 0

        lax.fori_loop(0, chips, arrived, 0)
        parts = [rx.at[s] for s in range(chips)]
        slot = 0
        while len(parts) > 1:
            pairs = list(zip(parts[::2], parts[1::2]))
            results = [joined(late[...], early[...]) for early, late in pairs]
            fresh = []
            for result in results:
                tree[slot] = result
                fresh.append(tree.at[slot])
                slot += 1
            parts = fresh + (parts[-1:] if len(parts) % 2 else [])

        @pl.when(seg == 0)
        def _():
            first_state[...] = applied(tree[chips - 2], init_ref[...])
            for g in range(segs - 1, 0, -1):
                fput(g).start()

        for g in range(segs - 1, 1, -1):

            @pl.when((seg > 0) & (seg < g))
            def _():
                zput(g).start()

        total[:, :dk] = jnp.where(iota((dk, dk), 0) == iota((dk, dk), 1), 1.0, 0.0).astype(F32)
        total[:, dk:] = jnp.zeros((dk, dv), F32)

        def one(s, _):
            so_far = total[...]
            prefix[s] = so_far
            total[...] = joined(rx[s], so_far)
            return 0

        lax.fori_loop(0, chips, one, 0)

        @pl.when(seg == 0)
        def _():
            state[...] = init_ref[...]

        @pl.when(seg > 0)
        def _():
            fput(0).wait_recv()
            state[...] = zstate[...]

        for g in range(1, segs - 1):

            @pl.when(g < seg)
            def _():
                zgot(g).wait_recv()
                state[...] = applied(zx[g], state[...])

        def give(k, _):
            turn = lax.rem(chip, 2) + (chips - 1) * (1 - lax.rem(chip, 2))
            s = lax.rem(chips - 1 - chip + k * turn, chips)
            ready = applied(prefix[s], state[...])

            @pl.when(s != chip)
            def _():
                outgoing[s] = ready
                sput(s, 0).start()

            @pl.when(near(s, chip))
            def _():
                sput(s, 1).start()

            @pl.when(s == chip)
            def _():
                own_state[mine] = ready

            return 0

        lax.fori_loop(0, chips, give, 0)

    def sent(c):
        for h in range(heads):
            mput(h, c).wait_send()

    for_core(sent)

    for h in range(heads):

        @pl.when(me != h * span)
        def _():
            put(h).wait_send()

    @pl.when(owner)
    def _():
        @pl.when(seg == 0)
        def _():
            for g in range(1, segs):
                fput(g).wait_send()

        for g in range(2, segs):

            @pl.when((seg > 0) & (seg < g))
            def _():
                zput(g).wait_send()

    def ordered(k):
        return lax.rem(mine + (k // per) + (k % per) * (heads // per), heads)

    @pl.when(core == 0)
    def _():
        for k in range(heads):
            h = ordered(k)

            @pl.when(me != h * span)
            def _():
                sgot(h).wait_recv()

            @pl.when(relayed(h))
            def _():
                rput(h).start()

    def closing(i, _):
        group = [ordered(i * 2 + d) for d in range(2)]

        @pl.when(core > 0)
        def _():
            for h in group:

                @pl.when(relayed(h))
                def _():
                    rput(h).wait_recv()

                @pl.when(jnp.logical_not(relayed(h)))
                def _():
                    sgot(h).wait_recv()

        states = [split(own_state[h]) for h in group]
        reads = [
            dot(reach[h], jnp.concatenate([hi, hi], 0)) + dot(reach[h, :, :dk], lo) + base[h]
            for h, (hi, lo) in zip(group, states)
        ]
        squares = [jnp.mean(read * read, axis=-1, keepdims=True) for read in reads]
        for h, read, square in zip(group, reads, squares):
            normed = read * lax.rsqrt(square + 1e-6) * gain_ref[pl.ds(h, 1), :]
            qf[pl.ds(h, read.shape[0], stride=heads), :] = normed
        return 0

    lax.fori_loop(0, heads // 2, closing, 0)
    out_ref[...] = qf[...].astype(BF16)

    for h in range(heads):

        @pl.when((core == 0) & relayed(h))
        def _():
            rput(h).wait_send()

    @pl.when(owner)
    def _():
        def done(s, _):
            @pl.when(s != chip)
            def _():
                sput(s, 0).wait_send()

            @pl.when(near(s, chip))
            def _():
                sput(s, 1).wait_send()

            return 0

        lax.fori_loop(0, chips, done, 0)


def per_device(seqs, segs, query_rows, key_rows, value_rows, out_gain, initial_state):
    _, tokens, heads, dk = query_rows.shape
    dv = value_rows.shape[-1]
    steps = tokens * REFL
    nblk = steps // BLK
    per = 2
    count = heads * nblk
    wide = dk + dv
    chips = seqs // CORES
    anywhere = pl.BlockSpec(memory_space=pl.ANY)
    vmem = pl.BlockSpec(memory_space=pltpu.VMEM)
    dma = pltpu.SemaphoreType.DMA
    out = pl.pallas_call(
        functools.partial(kernel, seqs, segs, heads, per),
        in_specs=[anywhere] * 5,
        out_specs=vmem,
        out_shape=pltpu.VMEM((tokens * heads, dv), BF16),
        scratch_shapes=[
            pltpu.VMEM((tokens * heads, dk), BF16),
            pltpu.VMEM((steps * heads, dk), BF16),
            pltpu.VMEM((steps * heads, dv), BF16),
            pltpu.VMEM((heads, dv), F32),
            pltpu.VMEM((dk, dv), F32),
            dma((5,)),
            pltpu.VMEM((tokens * heads, dk), F32),
            pltpu.VMEM((steps * heads, dk), F32),
            pltpu.VMEM((steps * heads, dv), F32),
            pltpu.VMEM((count * SUB, BLK), F32),
            pltpu.VMEM((count * SUB, BLK), F32),
            pltpu.VMEM((count, BLK, BLK), F32),
            pltpu.VMEM((count, 1, BLK), F32),
            pltpu.VMEM((heads, nblk, BLK, dk), BF16),
            pltpu.VMEM((heads, nblk, dk, wide), F32),
            pltpu.VMEM((heads, nblk, BLK, wide), BF16),
            pltpu.VMEM((heads, nblk, BLK, wide), BF16),
            pltpu.VMEM((heads, nblk, dk, wide), F32),
            pltpu.VMEM((CORES, heads, dk, wide), F32),
            pltpu.VMEM((heads, dk // CORES, wide), F32),
            pltpu.VMEM((heads, tokens, 2 * dk), BF16),
            pltpu.VMEM((heads, tokens, dv), F32),
            pltpu.VMEM((chips, dk, wide), F32),
            pltpu.VMEM((chips, dk, wide), F32),
            pltpu.VMEM((chips, dk, dv), F32),
            pltpu.VMEM((dk, wide), F32),
            pltpu.VMEM((chips - 1, dk, wide), F32),
            pltpu.VMEM((segs, dk, wide), F32),
            pltpu.VMEM((dk, dv), F32),
            pltpu.VMEM((dk, dv), F32),
            pltpu.VMEM((heads, dk, dv), F32),
            pltpu.VMEM((dk, dv), F32),
            dma((heads,)),
            dma((heads,)),
            dma((heads,)),
            dma((chips, CORES)),
            dma((segs,)),
            dma((segs,)),
            dma((chips, CORES)),
            dma((heads,)),
            dma((heads,)),
            dma((heads,)),
        ],
        compiler_params=pltpu.CompilerParams(collective_id=0, has_side_effects=True),
        name="delta_product",
    )(
        query_rows.reshape(tokens * heads, dk),
        key_rows.reshape(steps * heads, dk),
        value_rows.reshape(steps * heads, dv),
        out_gain,
        initial_state,
    )
    return out.reshape(1, tokens, heads, dv)


def solution(mesh):
    return jax.shard_map(
        functools.partial(per_device, mesh.shape["seq"], mesh.shape["seg"]),
        mesh=mesh,
        in_specs=(
            P("seg", "seq", None, None),
            P("seg", "seq", None, None, None),
            P("seg", "seq", None, None, None),
            P(),
            P(),
        ),
        out_specs=P("seg", "seq", None, None),
        check_vma=False,
    )
```

```python
import functools

import jax
import jax.numpy as jnp
from jax import lax
from jax.experimental import pallas as pl
from jax.experimental.pallas import tpu as pltpu
from jax.sharding import PartitionSpec as P

F32 = jnp.float32
BF16 = jnp.bfloat16
REFL = 2
CORES = 2
BLK = 128
SUB = 16
LANES = 128
MESH = pl.DeviceIdType.MESH


def dot(a, b):
    return lax.dot_general(a, b, (((1,), (0,)), ((), ())), preferred_element_type=F32)


def dot_bt(a, b):
    return lax.dot_general(a, b, (((1,), (1,)), ((), ())), preferred_element_type=F32)


def dot_at(a, b):
    return lax.dot_general(a, b, (((0,), (0,)), ((), ())), preferred_element_type=F32)


def split(x):
    high = x.astype(BF16)
    return high, (x - high.astype(F32)).astype(BF16)


def dot3(a, b):
    ah, al = a
    bh, bl = b
    rows, width = ah.shape[0], bh.shape[1]
    both = jnp.concatenate([ah, al], 0)
    if width <= LANES:
        full = dot(both, jnp.concatenate([bh, bl], 1))
        return full[:rows, :width] + (full[:rows, width:] + full[rows:, :width])
    full = dot(both, bh)
    return full[:rows] + (full[rows:] + dot(ah, bl))


def dot2(a, exact):
    rows = a[0].shape[0]
    full = dot(jnp.concatenate(a, 0), exact)
    return full[:rows] + full[rows:]


def iota(shape, axis):
    return lax.broadcasted_iota(jnp.int32, shape, axis)


def grouped(x, size, odd):
    return [x[g * size : (g + 1) * size] for g in range(odd, x.shape[0] // size, 2)]


def joined(late, early):
    dk = early.shape[0]
    after = compose(late[:, :dk], early)
    return jnp.concatenate([after[:, :dk], after[:, dk:] + late[:, dk:]], axis=1)


def invert_level(inv, low, size):
    half = BLK // 2
    paired = iota((half, BLK), 1) // size == 2 * (iota((half, BLK), 0) // size)
    high, rest = split(inv)
    under = jnp.where(paired, jnp.concatenate(grouped(low, size, 1), 0), 0.0)
    if 2 * size == BLK:
        part = dot3(split(under[:, :size]), (high[:size], rest[:size]))
    else:
        part = dot3(split(under), (high, rest))
    blank = jnp.zeros((size, BLK), F32)
    spread = []
    for g in range(half // size):
        spread += [blank, part[g * size : (g + 1) * size]]
    own = tuple(jnp.concatenate(grouped(x, size, 1), 0) for x in (high, rest))
    fill = dot3(own, split(jnp.concatenate(spread, 0)))
    even, odd = grouped(inv, size, 0), grouped(inv, size, 1)
    rows = []
    for g in range(half // size):
        rows += [even[g], odd[g] - fill[g * size : (g + 1) * size]]
    return jnp.concatenate(rows, 0)


def wide(x):
    return jnp.concatenate(split(x), 1)


def tall(x):
    return jnp.concatenate(split(x), 0)


def compose_split(left, right):
    lh, ll = left
    rh, rl = right
    return dot(jnp.concatenate([lh, ll], 1), jnp.concatenate([rh, rh], 0)) + dot(lh, rl)


def compose(left, right):
    return compose_split(split(left), split(right))


def grams(first, per, heads, nblk, kf, dsc, low, norm, kb):
    row, col = iota((BLK, BLK), 0), iota((BLK, BLK), 1)
    eye = row == col
    lane = iota((SUB, BLK), 1)
    at = [(first + n // nblk, n % nblk) for n in range(per * nblk)]
    products, squares = [], []
    for n, (h, c) in enumerate(at):
        key = kf[pl.ds(c * BLK * heads + h, BLK, stride=heads), :].astype(BF16)
        kb[h, c] = key
        products.append(dot_bt(key, key))
        yield
    for n, gram in enumerate(products):
        diag = jnp.where(eye, gram, 0.0)
        squares.append(jnp.sum(diag, axis=1, keepdims=True))
        norm[first * nblk + n] = lax.rsqrt(jnp.sum(diag, axis=0, keepdims=True) + 1e-6)
        yield
    for n, gram in enumerate(products):
        rcol = lax.rsqrt(squares[n] + 1e-6)
        lower = jnp.where(row > col, gram * (2.0 * rcol * rcol), 0.0)
        low[first * nblk + n] = lower
        packed = lower[:SUB]
        for g in range(1, BLK // SUB):
            packed = jnp.where(lane // SUB == g, lower[g * SUB : (g + 1) * SUB], packed)
        dsc[pl.ds(pl.multiple_of((first * nblk + n) * SUB, SUB), SUB), :] = packed
        yield


def substitute(first, count, dsc, nsc):
    lane = iota((count, BLK), 1)
    solved = []
    for i in range(SUB):
        line = dsc[pl.ds(first * SUB + i, count, stride=SUB), :]
        total = jnp.where(lane % SUB == i, 1.0, 0.0)
        for j in range(i):
            factor = jnp.take_along_axis(line, (lane // SUB) * SUB + j, axis=1)
            total = total - factor * solved[j]
        solved.append(total)
        nsc[pl.ds(first * SUB + i, count, stride=SUB), :] = total
        yield


def factors(beside, first, per, heads, nblk, vf, nsc, low, norm, kb, steps, scaled_hi, scaled_lo, before, both, core):
    dk = kb.shape[-1]
    eye = iota((BLK, BLK), 0) == iota((BLK, BLK), 1)
    lane = iota((SUB, BLK), 1)
    inverses = []
    base = first * nblk
    for n in range(per * nblk):
        packed = nsc[pl.ds(pl.multiple_of((base + n) * SUB, SUB), SUB), :]
        inverses.append(
            jnp.concatenate(
                [jnp.where(lane // SUB == g, packed, 0.0) for g in range(BLK // SUB)], axis=0
            )
        )
    size = SUB
    while size < BLK:
        for n in range(per * nblk):
            inverses[n] = invert_level(inverses[n], low[base + n], size)
            for _ in range(2):
                next(beside, None)
        size *= 2
    for _ in beside:
        pass

    count = per * nblk
    at = [(first + n // nblk, n % nblk) for n in range(count)]
    keys = [kb[h, c] for h, c in at]
    keys = [jnp.concatenate([key, key], 0) for key in keys]
    values = [vf[pl.ds(c * BLK * heads + h, BLK, stride=heads), :].astype(BF16) for h, c in at]
    rrows = [norm[base + n] for n in range(count)]
    doubled = [inv * (2.0 * rrow) for inv, rrow in zip(inverses, rrows)]
    updates = [dot(wide(d), jnp.concatenate([v, v], 0)) for d, v in zip(doubled, values)]
    weights = [dot(wide(d * rrow), key) for d, rrow, key in zip(doubled, rrows, keys)]
    scaled = [split(jnp.concatenate([w, u], axis=1)) for w, u in zip(weights, updates)]
    moved = [dot_at(key, jnp.concatenate(s, 0)) for key, s in zip(keys, scaled)]
    for (h, c), s in zip(at, scaled):
        scaled_hi[h, c] = s[0]
        scaled_lo[h, c] = s[1]
    unit = jnp.where(eye, 1.0, 0.0)
    nodes = [jnp.concatenate([unit - m[:, :dk], m[:, dk:]], axis=1) for m in moved]
    for n, (h, c) in enumerate(at):
        if c & (c + 1):
            steps[h, c] = nodes[n]
    nodes = [nodes[h * nblk : (h + 1) * nblk] for h in range(per)]
    reached = 1
    while len(nodes[0]) > 1:
        for h in range(per):
            before[first + h, reached] = nodes[h][0]
        nodes = [[joined(late, early) for early, late in zip(x[::2], x[1::2])] for x in nodes]
        reached *= 2
    for h in range(per):
        both[core, first + h] = nodes[h][0]


def readers(h, heads, nblk, qf, kb, steps, scaled_hi, scaled_lo, before, reach, base):
    dk = qf.shape[1]
    tok = BLK // REFL
    visible = iota((tok, BLK), 1) <= REFL * iota((tok, BLK), 0) + (REFL - 1)
    blocks = range(nblk)
    queries = [qf[pl.ds(c * tok * heads + h, tok, stride=heads), :] for c in blocks]
    scores = [dot_bt(queries[c].astype(BF16), kb[h, c]) for c in blocks]
    scores = [split(jnp.where(visible, score, 0.0)) for score in scores]
    reads = [compose_split(scores[c], (scaled_hi[h, c], scaled_lo[h, c])) for c in blocks]
    gone = [split(query - read[:, :dk]) for query, read in zip(queries, reads)]
    reach[h, :tok, :] = jnp.concatenate(gone[0], 1)
    base[h, :tok, :] = reads[0][:, dk:]
    so_far = None
    for c in range(1, nblk):
        rows = slice(c * tok, (c + 1) * tok)
        so_far = joined(steps[h, c - 1], so_far) if c & (c - 1) else before[h, c]
        moved = compose_split(gone[c], split(so_far))
        reach[h, rows, :] = wide(moved[:, :dk])
        base[h, rows, :] = moved[:, dk:] + reads[c][:, dk:]


def applied(step, state):
    dk = step.shape[0]
    return compose(step[:, :dk], state) + step[:, dk:]


def folding(h, both, reach, base):
    dk = both.shape[2]
    moved = compose_split((reach[h, :, :dk], reach[h, :, dk:]), split(both[0, h]))
    reach[h] = wide(moved[:, :dk])
    base[h] = base[h] + moved[:, dk:]


def kernel(
    seqs, segs, heads, per,
    q_any, k_any, v_any, gain_any, init_any, out_ref,
    q_ref, k_ref, v_ref, gain_ref, init_ref, in_sem,
    qf, kf, vf, dsc, nsc, low, norm, kb, steps, scaled_hi, scaled_lo, before, both, merged, reach, base,
    rx, prefix, outgoing, total, tree, zx, first_state, zstate, own_state, state,
    mput_sem, mgot_sem, put_sem, got_sem, zput_sem, zgot_sem, sput_sem, sgot_sem, rput_sem, rgot_sem,
):
    dk = init_ref.shape[0]
    dv = init_ref.shape[1]
    half = dk // CORES
    nblk = k_ref.shape[0] // (heads * BLK)
    span = seqs // heads
    chips = seqs // CORES
    me = lax.axis_index("seq")
    seg = lax.axis_index("seg")
    core = lax.rem(me, CORES)
    chip = me // CORES
    mate = me + 1 - 2 * core
    owner = lax.rem(me, span) == 0
    mine = me // span
    mine_rows = pl.ds(pl.multiple_of(core * half, half), half)

    def near(first, second):
        return (first != second) & ((first // 2 == second // 2) | (first % 2 == second % 2))

    def relayed(h):
        return jnp.logical_not(near(h * span // CORES, chip))

    loads = [
        pltpu.make_async_copy(src, dst, in_sem.at[i])
        for i, (src, dst) in enumerate(
            [
                (k_any, k_ref),
                (v_any, v_ref),
                (q_any, q_ref),
                (gain_any, gain_ref),
                (init_any.at[mine], init_ref),
            ]
        )
    ]
    for load in loads:
        load.start()
    barrier = pltpu.get_barrier_semaphore()
    for d in range(1, seqs):
        pl.semaphore_signal(
            barrier, inc=1,
            device_id={"seq": lax.rem(me + d, seqs), "seg": seg}, device_id_type=MESH,
        )
    for d in range(1, segs):
        pl.semaphore_signal(
            barrier, inc=1,
            device_id={"seq": me, "seg": lax.rem(seg + d, segs)}, device_id_type=MESH,
        )

    def copy(src, dst, put, got, to_seq, to_seg):
        return pltpu.make_async_remote_copy(
            src_ref=src, dst_ref=dst, send_sem=put, recv_sem=got,
            device_id={"seq": to_seq, "seg": to_seg}, device_id_type=MESH,
        )

    def mput(h, c):
        ref = both.at[c, h] if c == 0 else both.at[c, h, :half]
        return copy(ref, ref, mput_sem.at[h], mgot_sem.at[h], mate, seg)

    def for_core(action):
        for c in range(CORES):

            @pl.when(core == c)
            def _():
                action(c)

    def put(h):
        return copy(
            merged.at[h], rx.at[chip, mine_rows], put_sem.at[h], got_sem.at[chip, core], h * span, seg
        )

    def got(s, c):
        ref = rx.at[s, pl.ds(c * half, half)]
        return copy(ref, ref, put_sem.at[0], got_sem.at[s, c], s * CORES, seg)

    def sput(s, c):
        return copy(
            outgoing.at[s], own_state.at[mine], sput_sem.at[s, c], sgot_sem.at[mine], s * CORES + c, seg
        )

    def sgot(h):
        return copy(own_state.at[h], own_state.at[h], sput_sem.at[0, 0], sgot_sem.at[h], h * span, seg)

    def rput(h):
        return copy(own_state.at[h], own_state.at[h], rput_sem.at[h], rgot_sem.at[h], mate, seg)

    def zput(g):
        return copy(tree.at[chips - 2], zx.at[seg], zput_sem.at[g], zgot_sem.at[seg], me, g)

    def zgot(g):
        return copy(tree.at[chips - 2], zx.at[g], zput_sem.at[g], zgot_sem.at[g], me, g)

    def fput(g):
        return copy(first_state, zstate, zput_sem.at[g], zgot_sem.at[0], me, g)

    loads[0].wait()
    kf[...] = k_ref[...].astype(F32)

    def group_of(i):
        turn = lax.rem(i + 1 + mine // per, heads // per)
        return turn, [turn * per + lax.rem(mine + 1 + d, per) for d in range(per)]

    def prepared(first):
        yield from grams(first, per, heads, nblk, kf, dsc, low, norm, kb)
        yield from substitute(first * nblk, per * nblk, dsc, nsc)

    for _ in prepared(group_of(0)[0] * per):
        pass

    for load in loads[1:]:
        load.wait()
    vf[...] = v_ref[...].astype(F32)

    def local(i, _):
        turn, group = group_of(i)
        @pl.when(i + 1 < heads // per)
        def _():
            beside = prepared(group_of(i + 1)[0] * per)
            factors(beside, turn * per, per, heads, nblk, vf, nsc, low, norm, kb, steps, scaled_hi, scaled_lo, before, both, core)

        @pl.when(i + 1 == heads // per)
        def _():
            beside = iter(())
            factors(beside, turn * per, per, heads, nblk, vf, nsc, low, norm, kb, steps, scaled_hi, scaled_lo, before, both, core)

        @pl.when(i == 0)
        def _():
            pl.semaphore_wait(barrier, seqs + segs - 2)

        def exchange(c):
            for h in group:
                mput(h, c).start()

        for_core(exchange)
        return 0

    lax.fori_loop(0, heads // per, local, 0)

    def merging(group):
        def arrived(c):
            for h in group:
                mput(h, 1 - c).wait_recv()

        for_core(arrived)
        results = [joined(both[1, h, mine_rows], both[0, h]) for h in group]
        for h, result in zip(group, results):
            merged[h] = result

            @pl.when(me != h * span)
            def _():
                put(h).start()

            @pl.when(me == h * span)
            def _():
                rx[chip, mine_rows] = merged[h]

    def merging_all(i, _):
        merging(group_of(i)[1])
        return 0

    lax.fori_loop(0, heads // per - 1, merging_all, 0)

    def merging_one(d, _):
        merging([group_of(heads // per - 1)[0] * per + lax.rem(mine + 1 + d, per)])
        return 0

    lax.fori_loop(0, per, merging_one, 0)

    qf[...] = q_ref[...].astype(F32)

    def reading(h, _):
        readers(h, heads, nblk, qf, kb, steps, scaled_hi, scaled_lo, before, reach, base)
        return 0

    lax.fori_loop(0, heads, reading, 0)

    @pl.when(core > 0)
    def _():
        def fold(h, _):
            folding(h, both, reach, base)
            return 0

        lax.fori_loop(0, heads, fold, 0)

    @pl.when(owner)
    def _():
        def arrived(s, _):
            for c in range(CORES):

                @pl.when(s * CORES + c != me)
                def _():
                    got(s, c).wait_recv()

            return 0

        lax.fori_loop(0, chips, arrived, 0)
        parts = [rx.at[s] for s in range(chips)]
        slot = 0
        while len(parts) > 1:
            pairs = list(zip(parts[::2], parts[1::2]))
            results = [joined(late[...], early[...]) for early, late in pairs]
            fresh = []
            for result in results:
                tree[slot] = result
                fresh.append(tree.at[slot])
                slot += 1
            parts = fresh + (parts[-1:] if len(parts) % 2 else [])

        @pl.when(seg == 0)
        def _():
            first_state[...] = applied(tree[chips - 2], init_ref[...])
            for g in range(segs - 1, 0, -1):
                fput(g).start()

        for g in range(2, segs):

            @pl.when((seg > 0) & (seg < g))
            def _():
                zput(g).start()

        total[:, :dk] = jnp.where(iota((dk, dk), 0) == iota((dk, dk), 1), 1.0, 0.0).astype(F32)
        total[:, dk:] = jnp.zeros((dk, dv), F32)

        def one(s, _):
            so_far = total[...]
            prefix[s] = so_far
            total[...] = joined(rx[s], so_far)
            return 0

        lax.fori_loop(0, chips, one, 0)

        @pl.when(seg == 0)
        def _():
            state[...] = init_ref[...]

        @pl.when(seg > 0)
        def _():
            fput(0).wait_recv()
            state[...] = zstate[...]

        for g in range(1, segs - 1):

            @pl.when(g < seg)
            def _():
                zgot(g).wait_recv()
                state[...] = applied(zx[g], state[...])

        def give(k, _):
            turn = lax.rem(chip, 2) + (chips - 1) * (1 - lax.rem(chip, 2))
            s = lax.rem(chips - 1 - chip + k * turn, chips)
            ready = applied(prefix[s], state[...])

            @pl.when(s != chip)
            def _():
                outgoing[s] = ready
                sput(s, 0).start()

            @pl.when(near(s, chip))
            def _():
                sput(s, 1).start()

            @pl.when(s == chip)
            def _():
                own_state[mine] = ready

            return 0

        lax.fori_loop(0, chips, give, 0)

    def sent(c):
        for h in range(heads):
            mput(h, c).wait_send()

    for_core(sent)

    for h in range(heads):

        @pl.when(me != h * span)
        def _():
            put(h).wait_send()

    @pl.when(owner)
    def _():
        @pl.when(seg == 0)
        def _():
            for g in range(1, segs):
                fput(g).wait_send()

        for g in range(2, segs):

            @pl.when((seg > 0) & (seg < g))
            def _():
                zput(g).wait_send()

    def ordered(k):
        return lax.rem(mine + (k // per) + (k % per) * (heads // per), heads)

    @pl.when(core == 0)
    def _():
        for k in range(heads):
            h = ordered(k)

            @pl.when(me != h * span)
            def _():
                sgot(h).wait_recv()

            @pl.when(relayed(h))
            def _():
                rput(h).start()

    def closing(i, _):
        group = [ordered(i * 2 + d) for d in range(2)]

        @pl.when(core > 0)
        def _():
            for h in group:

                @pl.when(relayed(h))
                def _():
                    rput(h).wait_recv()

                @pl.when(jnp.logical_not(relayed(h)))
                def _():
                    sgot(h).wait_recv()

        states = [split(own_state[h]) for h in group]
        reads = [
            dot(reach[h], jnp.concatenate([hi, hi], 0)) + dot(reach[h, :, :dk], lo) + base[h]
            for h, (hi, lo) in zip(group, states)
        ]
        squares = [jnp.mean(read * read, axis=-1, keepdims=True) for read in reads]
        for h, read, square in zip(group, reads, squares):
            normed = read * lax.rsqrt(square + 1e-6) * gain_ref[pl.ds(h, 1), :]
            qf[pl.ds(h, read.shape[0], stride=heads), :] = normed
        return 0

    lax.fori_loop(0, heads // 2, closing, 0)
    out_ref[...] = qf[...].astype(BF16)

    for h in range(heads):

        @pl.when((core == 0) & relayed(h))
        def _():
            rput(h).wait_send()

    @pl.when(owner)
    def _():
        def done(s, _):
            @pl.when(s != chip)
            def _():
                sput(s, 0).wait_send()

            @pl.when(near(s, chip))
            def _():
                sput(s, 1).wait_send()

            return 0

        lax.fori_loop(0, chips, done, 0)


def per_device(seqs, segs, query_rows, key_rows, value_rows, out_gain, initial_state):
    _, tokens, heads, dk = query_rows.shape
    dv = value_rows.shape[-1]
    steps = tokens * REFL
    nblk = steps // BLK
    per = 2
    count = heads * nblk
    wide = dk + dv
    chips = seqs // CORES
    anywhere = pl.BlockSpec(memory_space=pl.ANY)
    vmem = pl.BlockSpec(memory_space=pltpu.VMEM)
    dma = pltpu.SemaphoreType.DMA
    out = pl.pallas_call(
        functools.partial(kernel, seqs, segs, heads, per),
        in_specs=[anywhere] * 5,
        out_specs=vmem,
        out_shape=pltpu.VMEM((tokens * heads, dv), BF16),
        scratch_shapes=[
            pltpu.VMEM((tokens * heads, dk), BF16),
            pltpu.VMEM((steps * heads, dk), BF16),
            pltpu.VMEM((steps * heads, dv), BF16),
            pltpu.VMEM((heads, dv), F32),
            pltpu.VMEM((dk, dv), F32),
            dma((5,)),
            pltpu.VMEM((tokens * heads, dk), F32),
            pltpu.VMEM((steps * heads, dk), F32),
            pltpu.VMEM((steps * heads, dv), F32),
            pltpu.VMEM((count * SUB, BLK), F32),
            pltpu.VMEM((count * SUB, BLK), F32),
            pltpu.VMEM((count, BLK, BLK), F32),
            pltpu.VMEM((count, 1, BLK), F32),
            pltpu.VMEM((heads, nblk, BLK, dk), BF16),
            pltpu.VMEM((heads, nblk, dk, wide), F32),
            pltpu.VMEM((heads, nblk, BLK, wide), BF16),
            pltpu.VMEM((heads, nblk, BLK, wide), BF16),
            pltpu.VMEM((heads, nblk, dk, wide), F32),
            pltpu.VMEM((CORES, heads, dk, wide), F32),
            pltpu.VMEM((heads, dk // CORES, wide), F32),
            pltpu.VMEM((heads, tokens, 2 * dk), BF16),
            pltpu.VMEM((heads, tokens, dv), F32),
            pltpu.VMEM((chips, dk, wide), F32),
            pltpu.VMEM((chips, dk, wide), F32),
            pltpu.VMEM((chips, dk, dv), F32),
            pltpu.VMEM((dk, wide), F32),
            pltpu.VMEM((chips - 1, dk, wide), F32),
            pltpu.VMEM((segs, dk, wide), F32),
            pltpu.VMEM((dk, dv), F32),
            pltpu.VMEM((dk, dv), F32),
            pltpu.VMEM((heads, dk, dv), F32),
            pltpu.VMEM((dk, dv), F32),
            dma((heads,)),
            dma((heads,)),
            dma((heads,)),
            dma((chips, CORES)),
            dma((segs,)),
            dma((segs,)),
            dma((chips, CORES)),
            dma((heads,)),
            dma((heads,)),
            dma((heads,)),
        ],
        compiler_params=pltpu.CompilerParams(collective_id=0, has_side_effects=True),
        name="delta_product",
    )(
        query_rows.reshape(tokens * heads, dk),
        key_rows.reshape(steps * heads, dk),
        value_rows.reshape(steps * heads, dv),
        out_gain,
        initial_state,
    )
    return out.reshape(1, tokens, heads, dv)


def solution(mesh):
    return jax.shard_map(
        functools.partial(per_device, mesh.shape["seq"], mesh.shape["seg"]),
        mesh=mesh,
        in_specs=(
            P("seg", "seq", None, None),
            P("seg", "seq", None, None, None),
            P("seg", "seq", None, None, None),
            P(),
            P(),
        ),
        out_specs=P("seg", "seq", None, None),
        check_vma=False,
    )
```
